512 devices in a mesh: expert: 64 (over x, y, z_lo), tensor: 8 (over z_hi, core).
Axes of the slice: x: 4, y: 4, z: 16 (z_hi: 4, z_lo: 4; z = z_hi * 4 + z_lo), core: 2. Of those that a mesh axis runs over, the one named last changes fastest.
Arguments:
- batch_one: bfloat16 [32768, 1536], P(('expert', 'tensor')), may hold values from -6 to 6
- batch_two: bfloat16 [32768, 1536], P(('expert', 'tensor')), may hold values from -6 to 6
- norm_gain: bfloat16 [1536], replicated, may hold values from 0.25 to 1.75
- slots_one: int32 [32768, 8], P(('expert', 'tensor')), may hold values from 0 to 63, all different within a row; in each aligned block of 64 rows (0 to 63, 64 to 127, ...) at most 9 rows name the same one
- slots_two: int32 [32768, 8], P(('expert', 'tensor')), may hold values from 0 to 63, all different within a row; in each aligned block of 64 rows (0 to 63, 64 to 127, ...) at most 9 rows name the same one
- gates_one: float32 [32768, 8], P(('expert', 'tensor')), may hold values from 0.2 to 1
- gates_two: float32 [32768, 8], P(('expert', 'tensor')), may hold values from 0.2 to 1
- table_old: int32 [64], replicated, may hold values from 0 to 39, as said below
- table_new: int32 [64], replicated, may hold values from 0 to 39, as said below
- gate_old: bfloat16 [64, 1536, 512], P('expert', 'tensor'), as said below
- up_old: bfloat16 [64, 1536, 512], P('expert', 'tensor'), as said below
- down_old: bfloat16 [64, 512, 1536], P('expert', None, 'tensor'), as said below
Outputs:
- mixed_one: bfloat16 [32768, 1536], P(('expert', 'tensor'))
- mixed_two: bfloat16 [32768, 1536], P(('expert', 'tensor'))
The draws below stay inside these ranges and needn't reach their ends.
Inputs may be any that keep to these rules, and one draw needn't show every extreme that they name: `slots_one`: the 8 routes of a token name different slots; among the 64 tokens of one device no slot is named by more than 9 routes, a bound that some block reaches. `slots_two`: the 8 routes of a token name different slots; among the 64 tokens of one device no slot is named by more than 9 routes, a bound that some block reaches. `table_old`: when 64 >= 40 every expert is held by at least one slot; several slots may hold the same expert. table_new[s] equals table_old at slot s, s - 1 or s + 1 (modulo 64), and each of the three cases occurs. `gate_old`: slots that hold the same expert under table_old hold equal weights. `up_old`: slots that hold the same expert under table_old hold equal weights. `down_old`: slots that hold the same expert under table_old hold equal weights.
All inputs are finite; a program needn't handle non-finite values.
Results may differ from the reference program's by a relative error of at most 0.0071.
Values may be sent and summed in bfloat16 or wider, within the bound.
A program may use at most 128 MiB of HBM per device.

```python
import math
import jax
import jax.numpy as jnp
import numpy as np
from jax import lax

D = 1536
FF = 512
EXPERTS = 40
TOPK = 8
TOK = 64
SLOTS = 64
CAP = 9
TOKENS = 32768
N_EXPERT = 64
N_TENSOR = 8


def place_table(key):
    others = jax.random.permutation(jax.random.fold_in(key, 101), EXPERTS - 1).astype(jnp.int32)
    base = jnp.concatenate([jnp.full((1,), EXPERTS - 1, jnp.int32), others])
    if SLOTS > EXPERTS:
        extra = jax.random.randint(jax.random.fold_in(key, 102), (SLOTS - EXPERTS,), 0, EXPERTS - 1).astype(jnp.int32)
        base = jnp.concatenate([base, extra])
    held = base[:SLOTS]
    rest = jax.random.permutation(jax.random.fold_in(key, 103), SLOTS - 1).astype(jnp.int32) + 1
    order = jnp.concatenate([jnp.zeros((1,), jnp.int32), rest])
    return held[order].astype(jnp.int32)


def draw_table_old(key, part):
    return place_table(key)


def draw_table_new(key, part):
    table = place_table(key)
    offset = jax.random.randint(jax.random.fold_in(key, 104), (SLOTS,), -1, 2).astype(jnp.int32)
    offset = offset.at[0].set(-1).at[1].set(1).at[2].set(0)
    where_from = (jnp.arange(SLOTS, dtype=jnp.int32) + offset) % SLOTS
    return table[where_from].astype(jnp.int32)


def expert_weights(key, salt, shape, fan_in):
    table = place_table(key)
    values = jax.random.normal(jax.random.fold_in(key, salt), (EXPERTS,) + shape, jnp.float32) * fan_in ** (-0.5)
    return values[table].astype(jnp.bfloat16)


def draw_gate_old(key, part):
    return expert_weights(key, 201, (D, FF), D)


def draw_up_old(key, part):
    return expert_weights(key, 202, (D, FF), D)


def draw_down_old(key, part):
    return expert_weights(key, 203, (FF, D), FF)


def block_levels(own_key, dims, shards, smallest, top_value):
    factor_of, own = 1.0, jax.random.fold_in(own_key, 6)
    for position, blocks in shards:
        heights = jnp.exp(jax.random.uniform(jax.random.fold_in(own, position), (blocks,), jnp.float32, smallest / len(shards), top_value / len(shards)))
        factor_of = factor_of * jnp.repeat(heights, dims[position] // blocks).reshape([-1 if axis == position else 1 for axis in range(len(dims))])
    return factor_of


def assign_block(stream_key, own, number, rows, count, top, limit, skew):
    sequence = jax.random.permutation(stream_key, count)
    crowded, ordinary = portions_of(count, rows * top, limit, skew, True), portions_of(count, rows * top, limit, skew, False)
    places = jnp.arange(count)

    def named(lengths, rotation):
        used = int((lengths > 0).sum())
        fixed = max(1, used // 4)
        shifted = fixed + (places - fixed + rotation * (used - fixed)) % max(1, count - fixed)
        return jnp.zeros((count,), jnp.int32).at[sequence[jnp.where(places < fixed, places, shifted)]].set(jnp.asarray(lengths, jnp.int32))

    lengths = jnp.where(number % 4 == 0, named(crowded, number // 4), named(ordinary, number - number // 4 - 1))
    mixed = jax.random.permutation(jax.random.fold_in(own, 3), count)
    source_of, receiver = mixed[0:count // 2 * 2:2], mixed[1:count // 2 * 2:2]
    slack = jnp.minimum(lengths[source_of] - 1, limit - lengths[receiver]) // 2
    slack = jnp.where((source_of == sequence[0]) | (receiver == sequence[0]) | (lengths[receiver] == 0), 0, jnp.maximum(slack, 0))
    shifted = jax.random.randint(jax.random.fold_in(own, 4), (count // 2,), 0, 1 << 20) % (slack + 1)
    lengths = lengths.at[source_of].add(-shifted).at[receiver].add(shifted)
    items = jnp.searchsorted(jnp.cumsum(lengths), jnp.arange(rows * top), side="right").astype(jnp.int32)
    grid = items.reshape(top, rows).T
    grid = grid[jax.random.permutation(jax.random.fold_in(own, 1), rows)]
    rotation = jax.random.randint(jax.random.fold_in(own, 2), (rows, 1), 0, top)
    return jnp.take_along_axis(grid, (jnp.arange(top)[None, :] + rotation) % top, axis=1)


def portions_of(count, total, limit, lean, full):
    loads = [(1 << 20) // math.isqrt(rank ** lean) + 1 for rank in range(1, count + 1)]
    largest = limit if full else min(limit, max(-(-total // count), total * loads[0] // sum(loads)))
    least = 1 if total - largest >= count - 1 else 0
    given, spare = [largest] + [least] * (count - 1), total - largest - least * (count - 1)
    while spare > 0:
        candidates = [i for i in range(1, count) if given[i] < largest] or [i for i in range(1, count) if given[i] < limit]
        whole, left = sum([loads[i] for i in candidates]), spare
        for i in candidates:
            addition = min(limit - given[i], max(1, left * loads[i] // whole), spare)
            given[i] = given[i] + addition
            spare = spare - addition
    return np.array(given)


def noise(key, dims, deviation, most, pieces=(), held_as=jnp.bfloat16):
    level = block_levels(key, dims, pieces, -0.22, 0.18) if pieces else 1.0
    values = jax.random.normal(key, dims, jnp.float32) * deviation * level
    return jnp.minimum(jnp.maximum(values, -most), most).astype(held_as)


def setup_inputs(seed: int = 0) -> dict:
    keys = jax.random.split(jax.random.key(seed), 13)
    batch_one = noise(keys[0], (TOKENS, D), 1.0, 6.0, ((0, 512),))
    batch_two = noise(keys[1], (TOKENS, D), 1.0, 6.0, ((0, 512),))
    norm_gain = jnp.clip(1.0 + 0.15 * jax.random.normal(keys[2], (D,), jnp.float32), 0.25, 1.75).astype(jnp.bfloat16)
    slots_one_keys = jax.random.split(jax.random.fold_in(keys[3], 1), TOKENS // TOK)
    slots_one_turns = jax.random.permutation(jax.random.fold_in(keys[3], 3), TOKENS // TOK)
    slots_one = jax.vmap(lambda own, number: assign_block(jax.random.fold_in(keys[3], 2), own, number, TOK, SLOTS, TOPK, CAP, 2))(slots_one_keys, slots_one_turns).reshape((TOKENS, TOPK))
    slots_two_keys = jax.random.split(jax.random.fold_in(keys[4], 1), TOKENS // TOK)
    slots_two_turns = jax.random.permutation(jax.random.fold_in(keys[4], 3), TOKENS // TOK)
    slots_two = jax.vmap(lambda own, number: assign_block(jax.random.fold_in(keys[4], 2), own, number, TOK, SLOTS, TOPK, CAP, 2))(slots_two_keys, slots_two_turns).reshape((TOKENS, TOPK))
    gates_one = jnp.clip(0.2 + 0.8 * jax.random.uniform(keys[5], (TOKENS, TOPK), jnp.float32) ** block_levels(keys[5], (TOKENS, TOPK), ((0, 512),), -0.2, 0.2), 0.2, 1.0)
    gates_two = jnp.clip(0.2 + 0.8 * jax.random.uniform(keys[6], (TOKENS, TOPK), jnp.float32) ** block_levels(keys[6], (TOKENS, TOPK), ((0, 512),), -0.2, 0.2), 0.2, 1.0)
    table_old = draw_table_old(jax.random.fold_in(keys[12], 71), 0)
    table_new = draw_table_new(jax.random.fold_in(keys[12], 71), 0)
    gate_old = draw_gate_old(jax.random.fold_in(keys[12], 71), 0)
    up_old = draw_up_old(jax.random.fold_in(keys[12], 71), 0)
    down_old = draw_down_old(jax.random.fold_in(keys[12], 71), 0)
    return {"batch_one": batch_one, "batch_two": batch_two, "norm_gain": norm_gain, "slots_one": slots_one, "slots_two": slots_two, "gates_one": gates_one, "gates_two": gates_two, "table_old": table_old, "table_new": table_new, "gate_old": gate_old, "up_old": up_old, "down_old": down_old}


EPS = 1e-05

def rms_rows(tokens, norm_gain):
    values = tokens.astype(jnp.float32)
    square = lax.optimization_barrier(jnp.mean(values * values, axis=-1, keepdims=True))
    return (values * lax.rsqrt(square + EPS) * norm_gain.astype(jnp.float32)).astype(jnp.bfloat16)

def source_slots(table_old, table_new):
    group = table_old.shape[0]
    slot_index = jnp.arange(group, dtype=jnp.int32)
    left_table = jnp.roll(table_old, 1)
    picked = jnp.where(table_new == left_table, (slot_index - 1) % group, (slot_index + 1) % group)
    return jnp.where(table_new == table_old, slot_index, picked).astype(jnp.int32)

def expert_mix(normed, route_slots, route_gates, gate_weights, up_weights, down_weights):
    tok_total = normed.shape[0]
    flat_slot = route_slots.reshape(-1)
    flat_gate = route_gates.reshape(-1)
    flat_token = (jnp.arange(flat_slot.shape[0], dtype=jnp.int32) // TOPK).astype(jnp.int32)
    bound = N_EXPERT * N_TENSOR * CAP

    def visit(total, inputs):
        slot_index, gate_slot, up_slot, down_slot = inputs
        chosen = flat_slot == slot_index
        found = jnp.sum(chosen.astype(jnp.int32))
        entry = jnp.nonzero(chosen, size=bound, fill_value=0)[0].astype(jnp.int32)
        valid = jnp.arange(bound, dtype=jnp.int32) < found
        token_ids = flat_token[entry]
        weight = jnp.where(valid, flat_gate[entry], jnp.zeros_like(flat_gate[entry]))
        row_block = normed[token_ids]
        gate_act = jnp.dot(row_block, gate_slot, preferred_element_type=jnp.float32)
        up_act = jnp.dot(row_block, up_slot, preferred_element_type=jnp.float32)
        hidden = (jax.nn.silu(gate_act) * up_act).astype(jnp.bfloat16)
        result = jnp.dot(hidden, down_slot, preferred_element_type=jnp.float32).astype(jnp.bfloat16)
        total = total.at[token_ids].add(weight[:, None] * result.astype(jnp.float32))
        return (total, valid)
    start = jnp.zeros((tok_total, normed.shape[1]), jnp.float32)
    slot_ids = jnp.arange(gate_weights.shape[0], dtype=jnp.int32)
    total, ignored = lax.scan(visit, start, (slot_ids, gate_weights, up_weights, down_weights))
    return total.astype(jnp.bfloat16)

def reference(batch_one, batch_two, norm_gain, slots_one, slots_two, gates_one, gates_two, table_old, table_new, gate_old, up_old, down_old):
    mixed_one = expert_mix(rms_rows(batch_one, norm_gain), slots_one, gates_one, gate_old, up_old, down_old)
    source = source_slots(table_old, table_new)
    mixed_two = expert_mix(rms_rows(batch_two, norm_gain), slots_two, gates_two, gate_old[source], up_old[source], down_old[source])
    return (mixed_one, mixed_two)
```

```python
import functools

import jax
import jax.numpy as jnp
from jax import lax
from jax.experimental import pallas as pl
from jax.experimental.pallas import tpu as pltpu
from jax.sharding import PartitionSpec as P

EPS = 1e-05
MESH = pl.DeviceIdType.MESH
BF16 = jnp.bfloat16
F32 = jnp.float32

LINE = 4
PLANE = 16
HIGH = 4
ROWS = 40
PAD = 48
GROUP = 4


def body(
    x1, x2, gain, r1, r2, told, tnew, gate_in, up_in, down_in,
    o1, o2,
    wg, wu, wd, xg, rg, outg, recv, res, back, pick, part, precv, tgt, gat,
    ring_s, ring_r, far_s, far_r, sib_s, sib_r, nbr_s, nbr_r,
    zx_s, zx_r, zr_s, zr_r, a_s, a_r, a_l, b_s, b_r, b_l, p_s, p_r,
):
    e = lax.axis_index("expert")
    t = lax.axis_index("tensor")
    experts = lax.axis_size("expert")
    tensors = lax.axis_size("tensor")
    zl = e % LINE
    p = e // LINE
    zh = t // 2
    c = t % 2
    right = (e, (t + 2) % tensors)
    left = (e, (t + tensors - 2) % tensors)
    sibling = (e, zh * 2 + (1 - c))
    up_hop = (zl + 1) // LINE
    down_hop = 1 - (zl + LINE - 1) // LINE
    after = ((e + 1) % experts, (t + 2 * up_hop) % tensors)
    before = ((e + experts - 1) % experts, (t + tensors - 2 * down_hop) % tensors)
    weights = (wg, wu, wd)
    tokens, features = x1.shape

    def remote(src, dst, ss, rs, device):
        return pltpu.make_async_remote_copy(
            src_ref=src, dst_ref=dst, send_sem=ss, recv_sem=rs,
            device_id=device, device_id_type=MESH,
        )

    blank = jnp.zeros((PLANE, 16, features), BF16)
    for b in range(2):
        recv[b, :, PAD - 16:PAD, :] = blank
        back[b, :, PAD - 16:PAD, :] = blank

    barrier = pltpu.get_barrier_semaphore()

    def greet(device):
        pl.semaphore_signal(barrier, inc=1, device_id=device, device_id_type=MESH)

    for device in (right, left, sibling, after, before):
        greet(device)
    for o in range(1, LINE):
        greet((p * LINE + (zl + o) % LINE, t))

    def greet_plane(o, carry):
        greet((((p + o) % PLANE) * LINE + zl, t))
        return carry

    lax.fori_loop(1, PLANE, greet_plane, 0)
    pl.semaphore_wait(barrier, 5 + LINE - 1 + PLANE - 1)

    for w, shard in zip(weights, (gate_in, up_in, down_in)):
        w[0, zh, c] = shard[...]

    def ring(m, way):
        w = weights[m]
        return remote(
            w.at[0, zh, c], w.at[0, zh, c], ring_s.at[m, way], ring_r.at[m, way],
            (right, left)[way],
        )

    def far(m, way):
        w = weights[m]
        owner = (zh + HIGH - 1) % HIGH if way == 0 else (zh + 1) % HIGH
        half = pl.ds(way * (w.shape[3] // 2), w.shape[3] // 2)
        place = w.at[0, owner, c, half]
        return remote(place, place, far_s.at[m, way], far_r.at[m, way], (right, left)[way])

    def sib(v, m):
        w = weights[m]
        place = w.at[v, :, c]
        return remote(place, place, sib_s.at[v, m], sib_r.at[v, m], sibling)

    def nbr(m, way):
        w = weights[m]
        return remote(
            w.at[0, :, c], w.at[1 + way, :, c], nbr_s.at[m, way], nbr_r.at[m, way],
            (after, before)[way],
        )

    for m in range(3):
        for way in range(2):
            ring(m, way).start()

    def line_x(b, o):
        return remote(
            xg.at[b, zl], xg.at[b, zl], zx_s.at[b, o], zx_r.at[b, zl],
            (p * LINE + (zl + o) % LINE, t),
        )

    def line_r(b, o):
        return remote(
            rg.at[b, zl], rg.at[b, zl], zr_s.at[b, o], zr_r.at[b, zl],
            (p * LINE + (zl + o) % LINE, t),
        )

    def line_x_in(b, o):
        i = (zl + o) % LINE
        return remote(xg.at[b, i], xg.at[b, i], zx_s.at[b, o], zx_r.at[b, i], (p * LINE + i, t))

    def line_r_in(b, o):
        i = (zl + o) % LINE
        return remote(rg.at[b, i], rg.at[b, i], zr_s.at[b, o], zr_r.at[b, i], (p * LINE + i, t))

    scale = gain[...].astype(F32)
    for b, (x, r) in enumerate(((x1, r1), (x2, r2))):
        values = x[...].astype(F32)
        square = jnp.mean(values * values, axis=-1, keepdims=True)
        xg[b, zl] = (values * lax.rsqrt(square + EPS) * scale).astype(BF16)
        rg[b, zl] = r[...]
        for o in range(1, LINE):
            line_x(b, o).start()
            line_r(b, o).start()

    def block_send(b, d, src, dst, ss, rs, ls):
        @pl.when(d != p)
        def _():
            remote(
                src.at[b, d, pl.ds(0, ROWS)], dst.at[b, p, pl.ds(0, ROWS)],
                ss.at[b, d], rs.at[b, p], (d * LINE + zl, t),
            ).start()

        @pl.when(d == p)
        def _():
            pltpu.make_async_copy(
                src.at[b, d, pl.ds(0, ROWS)], dst.at[b, p, pl.ds(0, ROWS)], ls.at[b]
            ).start()

    def block_wait(b, src, dst, ss, rs, ls, which):
        def one(o, carry):
            d = (p + o) % PLANE
            copy = remote(
                src.at[b, d, pl.ds(0, ROWS)], dst.at[b, d, pl.ds(0, ROWS)],
                ss.at[b, d], rs.at[b, d], (d * LINE + zl, t),
            )
            if which == "in":
                copy.wait_recv()
            else:
                copy.wait_send()
            return carry

        lax.fori_loop(1, PLANE, one, 0)
        if which == "in":
            pltpu.make_async_copy(
                src.at[b, p, pl.ds(0, ROWS)], dst.at[b, p, pl.ds(0, ROWS)], ls.at[b]
            ).wait()

    def route(b):
        ids = (lax.broadcasted_iota(jnp.int32, (PLANE, tokens), 0) * LINE + zl).astype(F32)
        first = lax.broadcasted_iota(jnp.int32, (tokens, tokens), 0)
        second = lax.broadcasted_iota(jnp.int32, (tokens, tokens), 1)
        ahead = jnp.where(first < second, 1.0, 0.0).astype(BF16)
        targets, gates = [], []
        for i in range(LINE):
            info = rg[b, i]
            named = jnp.zeros((PLANE, tokens), F32)
            gate = jnp.zeros((PLANE, tokens), F32)
            for k in range(8):
                same = info[k:k + 1, :] == ids
                named = named + jnp.where(same, 1.0, 0.0)
                gate = gate + jnp.where(same, info[8 + k:9 + k, :], 0.0)
            rank = jnp.dot(named.astype(BF16), ahead, preferred_element_type=F32)
            targets.append(jnp.where(named > 0.5, rank * LINE + i, -1.0))
            gates.append(gate)
        tgt[b] = jnp.concatenate(targets, axis=1)
        gat[b] = jnp.concatenate(gates, axis=1)

    places = lax.broadcasted_iota(jnp.int32, (PAD, LINE * tokens), 0).astype(F32)

    def dispatch(b):
        route(b)
        for d in range(PLANE):
            pick[d] = jnp.where(tgt[b, d:d + 1, :] == places, 1.0, 0.0).astype(BF16)

        def group(q, carry):
            rows = pick[pl.ds(q * GROUP, GROUP)].reshape(GROUP * PAD, LINE * tokens)
            block = jnp.dot(
                rows, xg[b].reshape(LINE * tokens, features), preferred_element_type=F32
            ).astype(BF16)
            outg[b, pl.ds(q * GROUP, GROUP)] = block.reshape(GROUP, PAD, features)
            for j in range(GROUP):
                block_send(b, q * GROUP + j, outg, recv, a_s, a_r, a_l)
            return carry

        lax.fori_loop(0, PLANE // GROUP, group, 0)

    for b in range(2):
        for o in range(1, LINE):
            line_x_in(b, o).wait_recv()
            line_r_in(b, o).wait_recv()
        dispatch(b)

    def ring_in(m, way):
        w = weights[m]
        owner = (zh + HIGH - 1) % HIGH if way == 0 else (zh + 1) % HIGH
        place = w.at[0, owner, c]
        return remote(place, place, ring_s.at[m, way], ring_r.at[m, way], (right, left)[way])

    def far_in(m, way):
        w = weights[m]
        half = pl.ds(way * (w.shape[3] // 2), w.shape[3] // 2)
        place = w.at[0, (zh + 2) % HIGH, c, half]
        return remote(place, place, far_s.at[m, way], far_r.at[m, way], (right, left)[way])

    def sib_in(v, m):
        w = weights[m]
        place = w.at[v, :, 1 - c]
        return remote(place, place, sib_s.at[v, m], sib_r.at[v, m], sibling)

    def nbr_in(m, way):
        w = weights[m]
        place = w.at[1 + way, :, c]
        return remote(place, place, nbr_s.at[m, way], nbr_r.at[m, way], (after, before)[way])

    for m in range(3):
        for way in range(2):
            ring_in(m, way).wait_recv()
            far(m, way).start()
    for m in range(3):
        for way in range(2):
            far_in(m, way).wait_recv()
        sib(0, m).start()
    for m in range(3):
        for way in range(2):
            nbr(m, way).start()
    for m in range(3):
        sib_in(0, m).wait_recv()

    def experts_on(b, v):
        inner = wg.shape[4]

        def group(q, carry):
            rows = recv[b, pl.ds(q * GROUP, GROUP)].reshape(GROUP * PAD, features)
            gate_act = jnp.dot(rows, wg[v].reshape(features, inner), preferred_element_type=F32)
            up_act = jnp.dot(rows, wu[v].reshape(features, inner), preferred_element_type=F32)
            hidden = (gate_act / (1.0 + jnp.exp(-gate_act)) * up_act).astype(BF16)
            result = lax.dot_general(
                hidden, wd[v].reshape(features, inner), (((1,), (1,)), ((), ())),
                preferred_element_type=F32,
            ).astype(BF16)
            res[b, pl.ds(q * GROUP, GROUP)] = result.reshape(GROUP, PAD, features)
            for j in range(GROUP):
                block_send(b, q * GROUP + j, res, back, b_s, b_r, b_l)
            return carry

        lax.fori_loop(0, PLANE // GROUP, group, 0)

    def part_out(b, o):
        i = (zl + o) % LINE
        return remote(
            part.at[b, i], precv.at[b, zl], p_s.at[b, o], p_r.at[b, zl], (p * LINE + i, t)
        )

    def part_in(b, o):
        i = (zl + o) % LINE
        return remote(
            part.at[b, i], precv.at[b, i], p_s.at[b, o], p_r.at[b, i], (p * LINE + i, t)
        )

    def combine(b):
        for d in range(PLANE):
            pick[d] = jnp.where(
                tgt[b, d:d + 1, :] == places, gat[b, d:d + 1, :], 0.0
            ).astype(BF16)
        mixer = pick[...].reshape(PLANE * PAD, LINE * tokens)
        total = lax.dot_general(
            mixer, back[b].reshape(PLANE * PAD, features), (((0,), (0,)), ((), ())),
            preferred_element_type=F32,
        ).astype(BF16)
        part[b] = total.reshape(LINE, tokens, features)
        for o in range(1, LINE):
            part_out(b, o).start()
        precv[b, zl] = part[b, zl]

    def finish(b, out):
        for o in range(1, LINE):
            part_in(b, o).wait_recv()
        total = precv[b, 0].astype(F32)
        for i in range(1, LINE):
            total = total + precv[b, i].astype(F32)
        out[...] = total.astype(BF16)

    block_wait(0, outg, recv, a_s, a_r, a_l, "in")
    experts_on(0, 0)
    block_wait(0, res, back, b_s, b_r, b_l, "in")
    combine(0)

    for m in range(3):
        for way in range(2):
            nbr_in(m, way).wait_recv()
            sib(1 + way, m).start()
    block_wait(1, outg, recv, a_s, a_r, a_l, "in")
    finish(0, o1)
    for m in range(3):
        for way in range(2):
            sib_in(1 + way, m).wait_recv()

    wanted = tnew[e]
    keeps = wanted == told[e]
    lower = wanted == told[(e + experts - 1) % experts]
    experts_on(1, jnp.where(keeps, 0, jnp.where(lower, 1, 2)))
    block_wait(1, res, back, b_s, b_r, b_l, "in")
    combine(1)
    finish(1, o2)

    for m in range(3):
        for way in range(2):
            ring(m, way).wait_send()
            far(m, way).wait_send()
            nbr(m, way).wait_send()
        for v in range(3):
            sib(v, m).wait_send()
    for b in range(2):
        for o in range(1, LINE):
            line_x(b, o).wait_send()
            line_r(b, o).wait_send()
            part_out(b, o).wait_send()
        block_wait(b, outg, recv, a_s, a_r, a_l, "out")
        block_wait(b, res, back, b_s, b_r, b_l, "out")


def local(
    batch_one, batch_two, norm_gain, slots_one, slots_two, gates_one, gates_two,
    table_old, table_new, gate_old, up_old, down_old,
):
    tokens, features = batch_one.shape
    shard, inner = gate_old.shape[1:]
    info = [
        jnp.concatenate([slots.astype(F32).T, gates.T], axis=0)
        for slots, gates in ((slots_one, gates_one), (slots_two, gates_two))
    ]
    vmem = pl.BlockSpec(memory_space=pltpu.VMEM)
    smem = pl.BlockSpec(memory_space=pltpu.SMEM)
    dma = pltpu.SemaphoreType.DMA
    full = pltpu.VMEM((3, HIGH, 2, shard, inner), BF16)
    blocks = pltpu.VMEM((2, PLANE, PAD, features), BF16)
    line = pltpu.VMEM((2, LINE, tokens, features), BF16)
    return pl.pallas_call(
        body,
        out_shape=[jax.ShapeDtypeStruct((tokens, features), BF16)] * 2,
        in_specs=[vmem] * 5 + [smem] * 2 + [vmem] * 3,
        out_specs=[vmem] * 2,
        scratch_shapes=[
            full, full, full,
            line, pltpu.VMEM((2, LINE, 16, tokens), F32),
            blocks, blocks, blocks, blocks,
            pltpu.VMEM((PLANE, PAD, LINE * tokens), BF16),
            line, line,
            pltpu.VMEM((2, PLANE, LINE * tokens), F32), pltpu.VMEM((2, PLANE, LINE * tokens), F32),
            dma((3, 2)), dma((3, 2)), dma((3, 2)), dma((3, 2)),
            dma((3, 3)), dma((3, 3)), dma((3, 2)), dma((3, 2)),
            dma((2, LINE)), dma((2, LINE)), dma((2, LINE)), dma((2, LINE)),
            dma((2, PLANE)), dma((2, PLANE)), dma((2,)),
            dma((2, PLANE)), dma((2, PLANE)), dma((2,)),
            dma((2, LINE)), dma((2, LINE)),
        ],
        compiler_params=pltpu.CompilerParams(
            collective_id=0, has_side_effects=True, vmem_limit_bytes=60 * 1024 * 1024
        ),
    )(
        batch_one, batch_two, norm_gain.reshape(1, features), info[0], info[1],
        table_old, table_new, gate_old[0], up_old[0], down_old[0].T,
    )


def solution(mesh):
    rows = P(("expert", "tensor"), None)
    in_specs = (
        rows, rows, P(), rows, rows, rows, rows, P(), P(),
        P("expert", "tensor", None), P("expert", "tensor", None), P("expert", None, "tensor"),
    )
    return jax.shard_map(
        local, mesh=mesh, in_specs=in_specs, out_specs=(rows, rows), check_vma=False
    )
```

```python
import functools

import jax
import jax.numpy as jnp
from jax import lax
from jax.experimental import pallas as pl
from jax.experimental.pallas import tpu as pltpu
from jax.sharding import PartitionSpec as P

EPS = 1e-05
MESH = pl.DeviceIdType.MESH
BF16 = jnp.bfloat16
F32 = jnp.float32

LINE = 4
DEPTH = 16
PLANE = 16
HIGH = 4
WIDE = 4
ROWS = 40
PAD = 48
HOPS = 11
WHOLE = 4
SHARED = (1, 3, 4, 5, 7, 8, 9, 11)
ORDER = (2, 1, 3, 0)


def body(
    x1, x2, gain, r1, r2, told, tnew, gate_in, up_in, down_in,
    o1, o2,
    wg, wu, wd, xg, rg, outg, recv, res, back, pick, part, precv, tgt, gat,
    ring_s, ring_r, own_s, own_r, sib_s, sib_r, edge_s, edge_r, esib_s, esib_r,
    zx_s, zx_r, zr_s, zr_r, a_s, a_r, a_l, b_s, b_r, b_l, p_s, p_r,
):
    e = lax.axis_index("expert")
    t = lax.axis_index("tensor")
    experts = lax.axis_size("expert")
    zl = e % HIGH
    p = e // HIGH
    px = p // WIDE
    py = p % WIDE
    zh = t // 2
    c = t % 2
    z = zh * HIGH + zl
    top = (zl + 1) // HIGH
    on_edge = zl % (HIGH - 1) == 0
    skip = 2 * (1 - 2 * (z % 2))
    sibling = (e, zh * 2 + (1 - c))
    weights = (wg, wu, wd)
    tokens, features = x1.shape
    shard, inner = gate_in.shape

    def along(distance):
        other = (z + distance + 2 * DEPTH) % DEPTH
        return (p * HIGH + other % HIGH, (other // HIGH) * 2 + c)

    def remote(src, dst, ss, rs, device):
        return pltpu.make_async_remote_copy(
            src_ref=src, dst_ref=dst, send_sem=ss, recv_sem=rs,
            device_id=device, device_id_type=MESH,
        )

    blank = jnp.zeros((PLANE, 16, features), BF16)
    for b in range(2):
        recv[b, :, PAD - 16:PAD, :] = blank
        back[b, :, PAD - 16:PAD, :] = blank

    barrier = pltpu.get_barrier_semaphore()

    def greet(device):
        pl.semaphore_signal(barrier, inc=1, device_id=device, device_id_type=MESH)

    for device in (along(1), along(-1), along(2), along(-2), sibling):
        greet(device)

    def greet_plane(o, carry):
        greet((((p + o) % PLANE) * HIGH + zl, t))
        return carry

    lax.fori_loop(1, PLANE, greet_plane, 0)
    pl.semaphore_wait(barrier, 5 + PLANE - 1)

    def spot(m, column, owner, hop, way):
        place = weights[m].at[column, owner // HIGH, c]
        if hop <= WHOLE:
            return place
        return place.at[pl.ds(pl.multiple_of(way * (shard // 2), shard // 2), shard // 2)]

    def source(hop, way):
        return (z - (1 - 2 * way) * hop + 2 * DEPTH) % DEPTH

    def ring(way, hop, m):
        owner = source(hop - 1, way)
        place = spot(m, owner % HIGH, owner, hop, way)
        return remote(
            place, place, ring_s.at[way, hop - 1, m], ring_r.at[way, hop - 1, m],
            along(1 - 2 * way),
        )

    def ring_in(way, hop, m):
        owner = source(hop, way)
        place = spot(m, owner % HIGH, owner, hop, way)
        return remote(
            place, place, ring_s.at[way, hop - 1, m], ring_r.at[way, hop - 1, m],
            along(1 - 2 * way),
        )

    def own(m):
        place = weights[m].at[zl, zh, c]
        return remote(place, place, own_s.at[m], own_r.at[m], sibling)

    def sib(way, hop, m):
        owner = source(hop, way)
        place = spot(m, owner % HIGH, owner, hop, way)
        k = SHARED.index(hop)
        return remote(place, place, sib_s.at[way, k, m], sib_r.at[way, k, m], sibling)

    def edge_way(hop):
        return top if hop % 4 == 1 else 1 - top

    def edge(hop, m):
        way = edge_way(hop)
        owner = source(hop, way)
        src = spot(m, owner % HIGH, owner, hop, way)
        dst = spot(m, HIGH, owner, hop, way)
        column = (e + HIGH * (1 - 2 * top) + experts) % experts
        k = hop // 2
        return remote(src, dst, edge_s.at[k, m], edge_r.at[k, m], (column, t))

    def esib(hop, m):
        way = edge_way(hop)
        owner = source(hop, way)
        place = spot(m, HIGH, owner, hop, way)
        k = hop // 2
        return remote(place, place, esib_s.at[k, m], esib_r.at[k, m], sibling)

    def edge_arrive(hop):
        @pl.when(on_edge)
        def _():
            for m in range(3):
                edge(hop, m).wait_recv()
                esib(hop, m).start()

    def tick(hop):
        for m in range(3):
            for way in range(2):
                ring_in(way, hop, m).wait_recv()
                if hop < HOPS:
                    ring(way, hop + 1, m).start()
        if hop % 2 == 1:
            @pl.when(on_edge)
            def _():
                for m in range(3):
                    edge(hop, m).start()
        if hop in SHARED:
            for m in range(3):
                for way in range(2):
                    sib(way, hop, m).start()
        if hop % 2 == 1 and hop > 1:
            edge_arrive(hop - 2)

    for w, mine in zip(weights, (gate_in, up_in, down_in)):
        w[zl, zh, c] = mine[...]
    for m in range(3):
        for way in range(2):
            ring(way, 1, m).start()
    for m in range(3):
        own(m).start()

    targets_of = (None, along(1), along(-1), along(skip))
    sources_of = (None, along(-1), along(1), along(-skip))

    def line_x(b, i):
        return remote(xg.at[b, 0], xg.at[b, i], zx_s.at[b, i], zx_r.at[b, i], targets_of[i])

    def line_r(b, i):
        return remote(rg.at[b, 0], rg.at[b, i], zr_s.at[b, i], zr_r.at[b, i], targets_of[i])

    def part_out(b, i):
        return remote(part.at[b, i], precv.at[b, i], p_s.at[b, i], p_r.at[b, i], sources_of[i])

    scale = gain[...].astype(F32)
    for b, (x, r) in enumerate(((x1, r1), (x2, r2))):
        values = x[...].astype(F32)
        square = jnp.mean(values * values, axis=-1, keepdims=True)
        xg[b, 0] = (values * lax.rsqrt(square + EPS) * scale).astype(BF16)
        rg[b, 0] = r[...]
        for i in range(1, LINE):
            line_x(b, i).start()
            line_r(b, i).start()

    def block_send(b, d, src, dst, ss, rs, ls):
        @pl.when(d != p)
        def _():
            remote(
                src.at[b, d, pl.ds(0, ROWS)], dst.at[b, p, pl.ds(0, ROWS)],
                ss.at[b, d], rs.at[b, p], (d * HIGH + zl, t),
            ).start()

        @pl.when(d == p)
        def _():
            pltpu.make_async_copy(
                src.at[b, d, pl.ds(0, ROWS)], dst.at[b, p, pl.ds(0, ROWS)], ls.at[b]
            ).start()

    def group_send(b, q, src, dst, ss, rs, ls):
        for k in ORDER:
            block_send(b, q * WIDE + (py + k) % WIDE, src, dst, ss, rs, ls)

    def block_wait(b, src, dst, ss, rs, ls, which):
        def one(o, carry):
            d = (p + o) % PLANE
            copy = remote(
                src.at[b, d, pl.ds(0, ROWS)], dst.at[b, d, pl.ds(0, ROWS)],
                ss.at[b, d], rs.at[b, d], (d * HIGH + zl, t),
            )
            if which == "in":
                copy.wait_recv()
            else:
                copy.wait_send()
            return carry

        lax.fori_loop(1, PLANE, one, 0)
        if which == "in":
            pltpu.make_async_copy(
                src.at[b, p, pl.ds(0, ROWS)], dst.at[b, p, pl.ds(0, ROWS)], ls.at[b]
            ).wait()

    def route(b):
        ids = (lax.broadcasted_iota(jnp.int32, (PLANE, tokens), 0) * HIGH + zl).astype(F32)
        first = lax.broadcasted_iota(jnp.int32, (tokens, tokens), 0)
        second = lax.broadcasted_iota(jnp.int32, (tokens, tokens), 1)
        ahead = jnp.where(first < second, 1.0, 0.0).astype(BF16)
        targets, gates = [], []
        for i in range(LINE):
            info = rg[b, i]
            named = jnp.zeros((PLANE, tokens), F32)
            gate = jnp.zeros((PLANE, tokens), F32)
            for k in range(8):
                same = info[k:k + 1, :] == ids
                named = named + jnp.where(same, 1.0, 0.0)
                gate = gate + jnp.where(same, info[8 + k:9 + k, :], 0.0)
            rank = jnp.dot(named.astype(BF16), ahead, preferred_element_type=F32)
            targets.append(jnp.where(named > 0.5, rank * LINE + i, -1.0))
            gates.append(gate)
        tgt[b] = jnp.concatenate(targets, axis=1)
        gat[b] = jnp.concatenate(gates, axis=1)

    places = lax.broadcasted_iota(jnp.int32, (PAD, LINE * tokens), 0).astype(F32)

    def dispatch(b):
        for i in range(1, LINE):
            line_x(b, i).wait_recv()
            line_r(b, i).wait_recv()
        route(b)
        for d in range(PLANE):
            pick[d] = jnp.where(tgt[b, d:d + 1, :] == places, 1.0, 0.0).astype(BF16)
        for k in ORDER:
            q = (px + k) % WIDE
            rows = pick[pl.ds(q * WIDE, WIDE)].reshape(WIDE * PAD, LINE * tokens)
            block = jnp.dot(
                rows, xg[b].reshape(LINE * tokens, features), preferred_element_type=F32
            ).astype(BF16)
            outg[b, pl.ds(q * WIDE, WIDE)] = block.reshape(WIDE, PAD, features)
            group_send(b, q, outg, recv, a_s, a_r, a_l)

    def experts_on(b, v, k):
        q = (px + k) % WIDE
        rows = recv[b, pl.ds(q * WIDE, WIDE)].reshape(WIDE * PAD, features)
        gate_act = jnp.dot(rows, wg[v].reshape(features, inner), preferred_element_type=F32)
        up_act = jnp.dot(rows, wu[v].reshape(features, inner), preferred_element_type=F32)
        hidden = (gate_act / (1.0 + jnp.exp(-gate_act)) * up_act).astype(BF16)
        result = lax.dot_general(
            hidden, wd[v].reshape(features, inner), (((1,), (1,)), ((), ())),
            preferred_element_type=F32,
        ).astype(BF16)
        res[b, pl.ds(q * WIDE, WIDE)] = result.reshape(WIDE, PAD, features)
        group_send(b, q, res, back, b_s, b_r, b_l)

    def combine(b):
        for d in range(PLANE):
            pick[d] = jnp.where(
                tgt[b, d:d + 1, :] == places, gat[b, d:d + 1, :], 0.0
            ).astype(BF16)
        mixer = pick[...].reshape(PLANE * PAD, LINE * tokens)
        total = lax.dot_general(
            mixer, back[b].reshape(PLANE * PAD, features), (((0,), (0,)), ((), ())),
            preferred_element_type=F32,
        ).astype(BF16)
        part[b] = total.reshape(LINE, tokens, features)
        for i in range(1, LINE):
            part_out(b, i).start()

    def finish(b, out):
        total = part[b, 0].astype(F32)
        for i in range(1, LINE):
            part_out(b, i).wait_recv()
            total = total + precv[b, i].astype(F32)
        out[...] = total.astype(BF16)

    dispatch(0)
    tick(1)
    dispatch(1)
    for hop in range(2, 9):
        tick(hop)

    block_wait(0, outg, recv, a_s, a_r, a_l, "in")
    for m in range(3):
        own(m).wait_recv()
        for hop in (4, 8):
            for way in range(2):
                sib(way, hop, m).wait_recv()
    experts_on(0, zl, 2)
    experts_on(0, zl, 1)
    tick(9)
    experts_on(0, zl, 3)
    experts_on(0, zl, 0)
    tick(10)
    tick(11)
    block_wait(1, outg, recv, a_s, a_r, a_l, "in")
    edge_arrive(11)
    for m in range(3):
        for hop in SHARED:
            if hop not in (4, 8):
                for way in range(2):
                    sib(way, hop, m).wait_recv()

    @pl.when(on_edge)
    def _():
        for m in range(3):
            for hop in range(1, HOPS + 1, 2):
                esib(hop, m).wait_recv()

    wanted = tnew[e]
    keeps = wanted == told[e]
    lower = wanted == told[(e + experts - 1) % experts]
    bottom = 1 - (zl + HIGH - 1) // HIGH
    column = jnp.where(
        keeps, zl, jnp.where(lower, zl - 1 + bottom * (HIGH + 1), zl + 1)
    )
    for k in ORDER:
        experts_on(1, column, k)
    block_wait(0, res, back, b_s, b_r, b_l, "in")
    combine(0)
    block_wait(1, res, back, b_s, b_r, b_l, "in")
    combine(1)
    finish(0, o1)
    finish(1, o2)

    for m in range(3):
        own(m).wait_send()
        for way in range(2):
            for hop in range(1, HOPS + 1):
                ring(way, hop, m).wait_send()
            for hop in SHARED:
                sib(way, hop, m).wait_send()

    @pl.when(on_edge)
    def _():
        for m in range(3):
            for hop in range(1, HOPS + 1, 2):
                edge(hop, m).wait_send()
                esib(hop, m).wait_send()

    for b in range(2):
        for i in range(1, LINE):
            line_x(b, i).wait_send()
            line_r(b, i).wait_send()
            part_out(b, i).wait_send()
        block_wait(b, outg, recv, a_s, a_r, a_l, "out")
        block_wait(b, res, back, b_s, b_r, b_l, "out")


def local(
    batch_one, batch_two, norm_gain, slots_one, slots_two, gates_one, gates_two,
    table_old, table_new, gate_old, up_old, down_old,
):
    tokens, features = batch_one.shape
    shard, inner = gate_old.shape[1:]
    info = [
        jnp.concatenate([slots.astype(F32).T, gates.T], axis=0)
        for slots, gates in ((slots_one, gates_one), (slots_two, gates_two))
    ]
    vmem = pl.BlockSpec(memory_space=pltpu.VMEM)
    smem = pl.BlockSpec(memory_space=pltpu.SMEM)
    dma = pltpu.SemaphoreType.DMA
    full = pltpu.VMEM((HIGH + 1, HIGH, 2, shard, inner), BF16)
    blocks = pltpu.VMEM((2, PLANE, PAD, features), BF16)
    line = pltpu.VMEM((2, LINE, tokens, features), BF16)
    return pl.pallas_call(
        body,
        out_shape=[jax.ShapeDtypeStruct((tokens, features), BF16)] * 2,
        in_specs=[vmem] * 5 + [smem] * 2 + [vmem] * 3,
        out_specs=[vmem] * 2,
        scratch_shapes=[
            full, full, full,
            line, pltpu.VMEM((2, LINE, 16, tokens), F32),
            blocks, blocks, blocks, blocks,
            pltpu.VMEM((PLANE, PAD, LINE * tokens), BF16),
            line, line,
            pltpu.VMEM((2, PLANE, LINE * tokens), F32), pltpu.VMEM((2, PLANE, LINE * tokens), F32),
            dma((2, HOPS, 3)), dma((2, HOPS, 3)), dma((3,)), dma((3,)),
            dma((2, len(SHARED), 3)), dma((2, len(SHARED), 3)),
            dma((6, 3)), dma((6, 3)), dma((6, 3)), dma((6, 3)),
            dma((2, LINE)), dma((2, LINE)), dma((2, LINE)), dma((2, LINE)),
            dma((2, PLANE)), dma((2, PLANE)), dma((2,)),
            dma((2, PLANE)), dma((2, PLANE)), dma((2,)),
            dma((2, LINE)), dma((2, LINE)),
        ],
        compiler_params=pltpu.CompilerParams(
            collective_id=0, has_side_effects=True, vmem_limit_bytes=60 * 1024 * 1024
        ),
    )(
        batch_one, batch_two, norm_gain.reshape(1, features), info[0], info[1],
        table_old, table_new, gate_old[0], up_old[0], down_old[0].T,
    )


def solution(mesh):
    rows = P(("expert", "tensor"), None)
    in_specs = (
        rows, rows, P(), rows, rows, rows, rows, P(), P(),
        P("expert", "tensor", None), P("expert", "tensor", None), P("expert", None, "tensor"),
    )
    return jax.shard_map(
        local, mesh=mesh, in_specs=in_specs, out_specs=(rows, rows), check_vma=False
    )
```

```python
import functools

import jax
import jax.numpy as jnp
from jax import lax
from jax.experimental import pallas as pl
from jax.experimental.pallas import tpu as pltpu
from jax.sharding import PartitionSpec as P

EPS = 1e-05
MESH = pl.DeviceIdType.MESH
BF16 = jnp.bfloat16
F32 = jnp.float32

LINE = 4
DEPTH = 16
PLANE = 16
HIGH = 4
WIDE = 4
ROWS = 40
PAD = 48
WHOLE = 4
HOPS = 9
REST = 10
SHARED = (1, 3, 4, 5, 7, 8, 9, REST)
EDGES = (1, 3, 5, 7, 9, REST)
ORDER = (2, 1, 3, 0)


def body(
    x1, x2, gain, s1, s2, g1, g2, told, tnew, gate_in, up_in, down_in,
    o1, o2,
    wg, wu, wd, xg, rg, outg, recv, res, back, pick, part, precv, tgt, gat,
    ring_s, ring_r, own_s, own_r, sib_s, sib_r, edge_s, edge_r, esib_s, esib_r,
    zx_s, zx_r, zr_s, zr_r, a_s, a_r, a_l, b_s, b_r, b_l, p_s, p_r,
):
    e = lax.axis_index("expert")
    t = lax.axis_index("tensor")
    experts = lax.axis_size("expert")
    zl = e % HIGH
    p = e // HIGH
    px = p // WIDE
    py = p % WIDE
    zh = t // 2
    c = t % 2
    z = zh * HIGH + zl
    top = (zl + 1) // HIGH
    on_edge = zl % (HIGH - 1) == 0
    skip = 2 * (1 - 2 * (z % 2))
    sibling = (e, zh * 2 + (1 - c))
    weights = (wg, wu, wd)
    shards = (gate_in, up_in, down_in)
    tokens, features = x1.shape
    shard, inner = gate_in.shape

    def along(distance):
        other = (z + distance + 2 * DEPTH) % DEPTH
        return (p * HIGH + other % HIGH, (other // HIGH) * 2 + c)

    def remote(src, dst, ss, rs, device):
        return pltpu.make_async_remote_copy(
            src_ref=src, dst_ref=dst, send_sem=ss, recv_sem=rs,
            device_id=device, device_id_type=MESH,
        )

    barrier = pltpu.get_barrier_semaphore()

    def greet(device):
        pl.semaphore_signal(barrier, inc=1, device_id=device, device_id_type=MESH)

    for device in (along(1), along(-1), along(2), along(-2), sibling):
        greet(device)

    def greet_plane(o, carry):
        greet((((p + o) % PLANE) * HIGH + zl, t))
        return carry

    lax.fori_loop(1, PLANE, greet_plane, 0)
    pl.semaphore_wait(barrier, 5 + PLANE - 1)

    def spot(m, column, owner, piece, way):
        place = weights[m].at[column, owner // HIGH, c]
        if piece <= WHOLE:
            return place
        half = 1 - way if piece == REST else way
        return place.at[pl.ds(pl.multiple_of(half * (shard // 2), shard // 2), shard // 2)]

    def source(piece, way, back_off=0):
        distance = (WHOLE + 1 if piece == REST else piece) - back_off
        return (z - (1 - 2 * way) * distance + 2 * DEPTH) % DEPTH

    def ring(way, piece, m):
        owner = source(piece, way, 1)
        place = spot(m, owner % HIGH, owner, piece, way)
        return remote(
            shards[m] if piece == 1 else place, place,
            ring_s.at[way, piece - 1, m], ring_r.at[way, piece - 1, m], along(1 - 2 * way),
        )

    def ring_in(way, piece, m):
        owner = source(piece, way)
        place = spot(m, owner % HIGH, owner, piece, way)
        return remote(
            place, place, ring_s.at[way, piece - 1, m], ring_r.at[way, piece - 1, m],
            along(1 - 2 * way),
        )

    def own(m):
        return remote(shards[m], weights[m].at[zl, zh, c], own_s.at[m], own_r.at[m], sibling)

    def own_in(m):
        return remote(
            shards[m], weights[m].at[zl, zh, 1 - c], own_s.at[m], own_r.at[m], sibling
        )

    def sib(way, piece, m):
        owner = source(piece, way)
        place = spot(m, owner % HIGH, owner, piece, way)
        k = SHARED.index(piece)
        return remote(place, place, sib_s.at[way, k, m], sib_r.at[way, k, m], sibling)

    def edge_way(piece):
        return 1 - top if piece % 4 == 3 else top

    def edge(piece, m):
        way = edge_way(piece)
        owner = source(piece, way)
        src = spot(m, owner % HIGH, owner, piece, way)
        dst = spot(m, HIGH, owner, piece, way)
        column = (e + HIGH * (1 - 2 * top) + experts) % experts
        k = EDGES.index(piece)
        return remote(src, dst, edge_s.at[k, m], edge_r.at[k, m], (column, t))

    def esib(piece, m):
        way = edge_way(piece)
        owner = source(piece, way)
        place = spot(m, HIGH, owner, piece, way)
        k = EDGES.index(piece)
        return remote(place, place, esib_s.at[k, m], esib_r.at[k, m], sibling)

    def edge_arrive(*pieces):
        @pl.when(on_edge)
        def _():
            for piece in pieces:
                for m in range(3):
                    edge(piece, m).wait_recv()
                    esib(piece, m).start()

    def tick(piece):
        for m in range(3):
            for way in range(2):
                ring_in(way, piece, m).wait_recv()
                if piece < HOPS:
                    ring(way, piece + 1, m).start()
        if piece == HOPS - 1:
            for m in range(3):
                for way in range(2):
                    ring(way, REST, m).start()
        if piece in EDGES:
            @pl.when(on_edge)
            def _():
                for m in range(3):
                    edge(piece, m).start()
        if piece in SHARED:
            for m in range(3):
                for way in range(2):
                    sib(way, piece, m).start()

    for m in range(3):
        for way in range(2):
            ring(way, 1, m).start()
    for m in range(3):
        own(m).start()

    targets_of = (None, along(1), along(-1), along(skip))
    sources_of = (None, along(-1), along(1), along(-skip))

    def line_x(b, i):
        return remote(xg.at[b, 0], xg.at[b, i], zx_s.at[b, i], zx_r.at[b, i], targets_of[i])

    def line_r(b, i):
        return remote(rg.at[b, 0], rg.at[b, i], zr_s.at[b, i], zr_r.at[b, i], targets_of[i])

    def part_out(b, i):
        return remote(part.at[b, i], precv.at[b, i], p_s.at[b, i], p_r.at[b, i], sources_of[i])

    scale = gain[...].astype(F32)
    for b, (x, slots, gates) in enumerate(((x1, s1, g1), (x2, s2, g2))):
        values = x[...].astype(F32)
        square = jnp.mean(values * values, axis=-1, keepdims=True)
        xg[b, 0] = (values * lax.rsqrt(square + EPS) * scale).astype(BF16)
        rg[b, 0, 0:8] = slots[...].astype(F32)
        rg[b, 0, 8:16] = gates[...]
        for i in range(1, LINE):
            line_x(b, i).start()
            line_r(b, i).start()

    for w, mine in zip(weights, shards):
        w[zl, zh, c] = mine[...]

    blank = jnp.zeros((PLANE, PAD - ROWS, features), BF16)
    for b in range(2):
        recv[b, :, ROWS:PAD, :] = blank
        back[b, :, ROWS:PAD, :] = blank

    def block_send(b, d, src, dst, ss, rs, ls):
        @pl.when(d != p)
        def _():
            remote(
                src.at[b, d, pl.ds(0, ROWS)], dst.at[b, p, pl.ds(0, ROWS)],
                ss.at[b, d], rs.at[b, p], (d * HIGH + zl, t),
            ).start()

        @pl.when(d == p)
        def _():
            pltpu.make_async_copy(
                src.at[b, d, pl.ds(0, ROWS)], dst.at[b, p, pl.ds(0, ROWS)], ls.at[b]
            ).start()

    def group_send(b, q, src, dst, ss, rs, ls):
        for k in ORDER:
            block_send(b, q * WIDE + (py + k) % WIDE, src, dst, ss, rs, ls)

    def block_wait(b, src, dst, ss, rs, ls, which):
        def one(o, carry):
            d = (p + o) % PLANE
            copy = remote(
                src.at[b, d, pl.ds(0, ROWS)], dst.at[b, d, pl.ds(0, ROWS)],
                ss.at[b, d], rs.at[b, d], (d * HIGH + zl, t),
            )
            if which == "in":
                copy.wait_recv()
            else:
                copy.wait_send()
            return carry

        lax.fori_loop(1, PLANE, one, 0)
        if which == "in":
            pltpu.make_async_copy(
                src.at[b, p, pl.ds(0, ROWS)], dst.at[b, p, pl.ds(0, ROWS)], ls.at[b]
            ).wait()

    def route(b):
        ids = (lax.broadcasted_iota(jnp.int32, (PLANE, tokens), 0) * HIGH + zl).astype(F32)
        first = lax.broadcasted_iota(jnp.int32, (tokens, tokens), 0)
        second = lax.broadcasted_iota(jnp.int32, (tokens, tokens), 1)
        ahead = jnp.where(first < second, 1.0, 0.0).astype(BF16)
        targets, gates = [], []
        for i in range(LINE):
            info = rg[b, i]
            named = jnp.zeros((PLANE, tokens), F32)
            gate = jnp.zeros((PLANE, tokens), F32)
            for k in range(8):
                same = info[k:k + 1, :] == ids
                named = named + jnp.where(same, 1.0, 0.0)
                gate = gate + jnp.where(same, info[8 + k:9 + k, :], 0.0)
            rank = jnp.dot(named.astype(BF16), ahead, preferred_element_type=F32)
            targets.append(jnp.where(named > 0.5, rank * LINE + i, -1.0))
            gates.append(gate)
        tgt[b] = jnp.concatenate(targets, axis=1)
        gat[b] = jnp.concatenate(gates, axis=1)

    places = lax.broadcasted_iota(jnp.int32, (PAD, LINE * tokens), 0).astype(F32)

    def dispatch(b):
        for i in range(1, LINE):
            line_x(b, i).wait_recv()
            line_r(b, i).wait_recv()
        route(b)
        for d in range(PLANE):
            pick[d] = jnp.where(tgt[b, d:d + 1, :] == places, 1.0, 0.0).astype(BF16)
        for k in ORDER:
            q = (px + k) % WIDE
            rows = pick[pl.ds(q * WIDE, WIDE)].reshape(WIDE * PAD, LINE * tokens)
            block = jnp.dot(
                rows, xg[b].reshape(LINE * tokens, features), preferred_element_type=F32
            ).astype(BF16)
            outg[b, pl.ds(q * WIDE, WIDE)] = block.reshape(WIDE, PAD, features)
            group_send(b, q, outg, recv, a_s, a_r, a_l)

    def experts_on(b, v, k):
        q = (px + k) % WIDE
        rows = recv[b, pl.ds(q * WIDE, WIDE)].reshape(WIDE * PAD, features)
        gate_act = jnp.dot(rows, wg[v].reshape(features, inner), preferred_element_type=F32)
        up_act = jnp.dot(rows, wu[v].reshape(features, inner), preferred_element_type=F32)
        hidden = (gate_act / (1.0 + jnp.exp(-gate_act)) * up_act).astype(BF16)
        result = lax.dot_general(
            hidden, wd[v].reshape(features, inner), (((1,), (1,)), ((), ())),
            preferred_element_type=F32,
        ).astype(BF16)
        res[b, pl.ds(q * WIDE, WIDE)] = result.reshape(WIDE, PAD, features)
        group_send(b, q, res, back, b_s, b_r, b_l)

    def combine(b):
        for d in range(PLANE):
            pick[d] = jnp.where(
                tgt[b, d:d + 1, :] == places, gat[b, d:d + 1, :], 0.0
            ).astype(BF16)
        mixer = pick[...].reshape(PLANE * PAD, LINE * tokens)
        total = lax.dot_general(
            mixer, back[b].reshape(PLANE * PAD, features), (((0,), (0,)), ((), ())),
            preferred_element_type=F32,
        ).astype(BF16)
        part[b] = total.reshape(LINE, tokens, features)
        for i in range(1, LINE):
            part_out(b, i).start()

    def finish(b, out):
        total = part[b, 0].astype(F32)
        for i in range(1, LINE):
            part_out(b, i).wait_recv()
            total = total + precv[b, i].astype(F32)
        out[...] = total

    dispatch(0)
    tick(1)
    dispatch(1)
    for piece in range(2, 7):
        tick(piece)
    edge_arrive(1)
    tick(7)
    tick(8)

    block_wait(0, outg, recv, a_s, a_r, a_l, "in")
    for m in range(3):
        own_in(m).wait_recv()
        for piece in (4, 8):
            for way in range(2):
                sib(way, piece, m).wait_recv()
    experts_on(0, zl, 2)
    experts_on(0, zl, 1)
    tick(9)
    experts_on(0, zl, 3)
    tick(REST)
    experts_on(0, zl, 0)
    block_wait(1, outg, recv, a_s, a_r, a_l, "in")
    edge_arrive(3, 5, 7, 9, REST)
    for m in range(3):
        for piece in SHARED:
            if piece not in (4, 8):
                for way in range(2):
                    sib(way, piece, m).wait_recv()

    @pl.when(on_edge)
    def _():
        for m in range(3):
            for piece in EDGES:
                esib(piece, m).wait_recv()

    wanted = tnew[e]
    keeps = wanted == told[e]
    lower = wanted == told[(e + experts - 1) % experts]
    bottom = 1 - (zl + HIGH - 1) // HIGH
    column = jnp.where(
        keeps, zl, jnp.where(lower, zl - 1 + bottom * (HIGH + 1), zl + 1)
    )
    for k in ORDER:
        experts_on(1, column, k)
    block_wait(0, res, back, b_s, b_r, b_l, "in")
    combine(0)
    block_wait(1, res, back, b_s, b_r, b_l, "in")
    combine(1)
    finish(0, o1)
    finish(1, o2)

    for m in range(3):
        own(m).wait_send()
        for way in range(2):
            for piece in range(1, REST + 1):
                ring(way, piece, m).wait_send()
            for piece in SHARED:
                sib(way, piece, m).wait_send()

    @pl.when(on_edge)
    def _():
        for m in range(3):
            for piece in EDGES:
                edge(piece, m).wait_send()
                esib(piece, m).wait_send()

    for b in range(2):
        for i in range(1, LINE):
            line_x(b, i).wait_send()
            line_r(b, i).wait_send()
            part_out(b, i).wait_send()
        block_wait(b, outg, recv, a_s, a_r, a_l, "out")
        block_wait(b, res, back, b_s, b_r, b_l, "out")


def local(
    batch_one, batch_two, norm_gain, slots_one, slots_two, gates_one, gates_two,
    table_old, table_new, gate_old, up_old, down_old,
):
    tokens, features = batch_one.shape
    shard, inner = gate_old.shape[1:]
    vmem = pl.BlockSpec(memory_space=pltpu.VMEM)
    smem = pl.BlockSpec(memory_space=pltpu.SMEM)
    dma = pltpu.SemaphoreType.DMA
    full = pltpu.VMEM((HIGH + 1, HIGH, 2, shard, inner), BF16)
    blocks = pltpu.VMEM((2, PLANE, PAD, features), BF16)
    line = pltpu.VMEM((2, LINE, tokens, features), BF16)
    one, two = pl.pallas_call(
        body,
        out_shape=[jax.ShapeDtypeStruct((tokens, features), F32)] * 2,
        in_specs=[vmem] * 7 + [smem] * 2 + [vmem] * 3,
        out_specs=[vmem] * 2,
        scratch_shapes=[
            full, full, full,
            line, pltpu.VMEM((2, LINE, 16, tokens), F32),
            blocks, blocks, blocks, blocks,
            pltpu.VMEM((PLANE, PAD, LINE * tokens), BF16),
            line, line,
            pltpu.VMEM((2, PLANE, LINE * tokens), F32), pltpu.VMEM((2, PLANE, LINE * tokens), F32),
            dma((2, REST, 3)), dma((2, REST, 3)), dma((3,)), dma((3,)),
            dma((2, len(SHARED), 3)), dma((2, len(SHARED), 3)),
            dma((6, 3)), dma((6, 3)), dma((6, 3)), dma((6, 3)),
            dma((2, LINE)), dma((2, LINE)), dma((2, LINE)), dma((2, LINE)),
            dma((2, PLANE)), dma((2, PLANE)), dma((2,)),
            dma((2, PLANE)), dma((2, PLANE)), dma((2,)),
            dma((2, LINE)), dma((2, LINE)),
        ],
        compiler_params=pltpu.CompilerParams(
            collective_id=0, has_side_effects=True, vmem_limit_bytes=60 * 1024 * 1024
        ),
    )(
        batch_one, batch_two, norm_gain, slots_one.T, slots_two.T, gates_one.T, gates_two.T,
        table_old, table_new, gate_old[0], up_old[0], down_old[0].T,
    )
    return one.astype(BF16), two.astype(BF16)


def solution(mesh):
    rows = P(("expert", "tensor"), None)
    in_specs = (
        rows, rows, P(), rows, rows, rows, rows, P(), P(),
        P("expert", "tensor", None), P("expert", "tensor", None), P("expert", None, "tensor"),
    )
    return jax.shard_map(
        local, mesh=mesh, in_specs=in_specs, out_specs=(rows, rows), check_vma=False
    )
```

```python
import functools

import jax
import jax.numpy as jnp
from jax import lax
from jax.experimental import pallas as pl
from jax.experimental.pallas import tpu as pltpu
from jax.sharding import PartitionSpec as P

EPS = 1e-05
MESH = pl.DeviceIdType.MESH
BF16 = jnp.bfloat16
F32 = jnp.float32

LINE = 4
DEPTH = 16
PLANE = 16
HIGH = 4
WIDE = 4
ROWS = 40
PAD = 48
WHOLE = 4
HOPS = 9
REST = 10
SHARED = (1, 3, 4, 5, 7, 8, 9, REST)
EDGES = (1, 3, 5, 7, 9, REST)
ORDER = (2, 1, 3, 0)
FAR_FIRST = sorted(
    ((dx, dy) for dx in range(WIDE) for dy in range(WIDE)),
    key=lambda d: (-min(d[0], WIDE - d[0]) - min(d[1], WIDE - d[1]), d),
)


def body(
    x1, x2, gain, s1, s2, g1, g2, told, tnew, gate_in, up_in, down_in,
    o1, o2,
    wg, wu, wd, xg, rg, outg, recv, res, back, pick, part, precv, tgt, gat,
    ring_s, ring_r, own_s, own_r, sib_s, sib_r, edge_s, edge_r, esib_s, esib_r,
    zx_s, zx_r, zr_s, zr_r, a_s, a_r, a_l, b_s, b_r, b_l, p_s, p_r,
):
    e = lax.axis_index("expert")
    t = lax.axis_index("tensor")
    experts = lax.axis_size("expert")
    zl = e % HIGH
    p = e // HIGH
    px = p // WIDE
    py = p % WIDE
    zh = t // 2
    c = t % 2
    z = zh * HIGH + zl
    top = (zl + 1) // HIGH
    on_edge = zl % (HIGH - 1) == 0
    skip = 2 * (1 - 2 * (z % 2))
    sibling = (e, zh * 2 + (1 - c))
    weights = (wg, wu, wd)
    shards = (gate_in, up_in, down_in)
    tokens, features = x1.shape
    shard, inner = gate_in.shape

    def along(distance):
        other = (z + distance + 2 * DEPTH) % DEPTH
        return (p * HIGH + other % HIGH, (other // HIGH) * 2 + c)

    def remote(src, dst, ss, rs, device):
        return pltpu.make_async_remote_copy(
            src_ref=src, dst_ref=dst, send_sem=ss, recv_sem=rs,
            device_id=device, device_id_type=MESH,
        )

    barrier = pltpu.get_barrier_semaphore()

    def greet(device):
        pl.semaphore_signal(barrier, inc=1, device_id=device, device_id_type=MESH)

    for device in (along(1), along(-1), along(2), along(-2), sibling):
        greet(device)

    def greet_plane(o, carry):
        greet((((p + o) % PLANE) * HIGH + zl, t))
        return carry

    lax.fori_loop(1, PLANE, greet_plane, 0)
    pl.semaphore_wait(barrier, 5 + PLANE - 1)

    def spot(m, column, owner, piece, way):
        place = weights[m].at[column, owner // HIGH, c]
        if piece <= WHOLE:
            return place
        half = 1 - way if piece == REST else way
        return place.at[pl.ds(pl.multiple_of(half * (shard // 2), shard // 2), shard // 2)]

    def source(piece, way, back_off=0):
        distance = (WHOLE + 1 if piece == REST else piece) - back_off
        return (z - (1 - 2 * way) * distance + 2 * DEPTH) % DEPTH

    def ring(way, piece, m):
        owner = source(piece, way, 1)
        place = spot(m, owner % HIGH, owner, piece, way)
        return remote(
            shards[m] if piece == 1 else place, place,
            ring_s.at[way, piece - 1, m], ring_r.at[way, piece - 1, m], along(1 - 2 * way),
        )

    def ring_in(way, piece, m):
        owner = source(piece, way)
        place = spot(m, owner % HIGH, owner, piece, way)
        return remote(
            place, place, ring_s.at[way, piece - 1, m], ring_r.at[way, piece - 1, m],
            along(1 - 2 * way),
        )

    def own(m):
        return remote(shards[m], weights[m].at[zl, zh, c], own_s.at[m], own_r.at[m], sibling)

    def own_in(m):
        return remote(
            shards[m], weights[m].at[zl, zh, 1 - c], own_s.at[m], own_r.at[m], sibling
        )

    def sib(way, piece, m):
        owner = source(piece, way)
        place = spot(m, owner % HIGH, owner, piece, way)
        k = SHARED.index(piece)
        return remote(place, place, sib_s.at[way, k, m], sib_r.at[way, k, m], sibling)

    def edge_way(piece):
        return 1 - top if piece % 4 == 3 else top

    def edge(piece, m):
        way = edge_way(piece)
        owner = source(piece, way)
        src = spot(m, owner % HIGH, owner, piece, way)
        dst = spot(m, HIGH, owner, piece, way)
        column = (e + HIGH * (1 - 2 * top) + experts) % experts
        k = EDGES.index(piece)
        return remote(src, dst, edge_s.at[k, m], edge_r.at[k, m], (column, t))

    def esib(piece, m):
        way = edge_way(piece)
        owner = source(piece, way)
        place = spot(m, HIGH, owner, piece, way)
        k = EDGES.index(piece)
        return remote(place, place, esib_s.at[k, m], esib_r.at[k, m], sibling)

    def edge_arrive(*pieces):
        @pl.when(on_edge)
        def _():
            for piece in pieces:
                for m in range(3):
                    edge(piece, m).wait_recv()
                    esib(piece, m).start()

    def tick(piece):
        for m in range(3):
            for way in range(2):
                ring_in(way, piece, m).wait_recv()
                if piece < HOPS:
                    ring(way, piece + 1, m).start()
        if piece == WHOLE:
            for m in range(3):
                for way in range(2):
                    ring(way, REST, m).start()
        if piece in EDGES:
            @pl.when(on_edge)
            def _():
                for m in range(3):
                    edge(piece, m).start()
        if piece in SHARED:
            for m in range(3):
                for way in range(2):
                    sib(way, piece, m).start()

    for m in range(3):
        for way in range(2):
            ring(way, 1, m).start()
    for m in range(3):
        own(m).start()

    targets_of = (None, along(1), along(-1), along(skip))
    sources_of = (None, along(-1), along(1), along(-skip))

    def line_x(b, i):
        return remote(xg.at[b, 0], xg.at[b, i], zx_s.at[b, i], zx_r.at[b, i], targets_of[i])

    def line_r(b, i):
        return remote(rg.at[b, 0], rg.at[b, i], zr_s.at[b, i], zr_r.at[b, i], targets_of[i])

    def part_out(b, i):
        return remote(part.at[b, i], precv.at[b, i], p_s.at[b, i], p_r.at[b, i], sources_of[i])

    scale = gain[...].astype(F32)
    for b, (x, slots, gates) in enumerate(((x1, s1, g1), (x2, s2, g2))):
        values = x[...].astype(F32)
        square = jnp.mean(values * values, axis=-1, keepdims=True)
        xg[b, 0] = (values * lax.rsqrt(square + EPS) * scale).astype(BF16)
        rg[b, 0, 0:8] = slots[...].astype(F32)
        rg[b, 0, 8:16] = gates[...]
        for i in range(1, LINE):
            line_x(b, i).start()
            line_r(b, i).start()

    for w, mine in zip(weights, shards):
        w[zl, zh, c] = mine[...]

    blank = jnp.zeros((PLANE, PAD - ROWS, features), BF16)
    for b in range(2):
        recv[b, :, ROWS:PAD, :] = blank
        back[b, :, ROWS:PAD, :] = blank

    def block_send(b, d, src, dst, ss, rs, ls):
        @pl.when(d != p)
        def _():
            remote(
                src.at[b, d, pl.ds(0, ROWS)], dst.at[b, p, pl.ds(0, ROWS)],
                ss.at[b, d], rs.at[b, p], (d * HIGH + zl, t),
            ).start()

        @pl.when(d == p)
        def _():
            pltpu.make_async_copy(
                src.at[b, d, pl.ds(0, ROWS)], dst.at[b, p, pl.ds(0, ROWS)], ls.at[b]
            ).start()

    def group_send(b, q, src, dst, ss, rs, ls):
        for k in ORDER:
            block_send(b, q * WIDE + (py + k) % WIDE, src, dst, ss, rs, ls)

    def block_wait(b, src, dst, ss, rs, ls, which):
        def one(o, carry):
            d = (p + o) % PLANE
            copy = remote(
                src.at[b, d, pl.ds(0, ROWS)], dst.at[b, d, pl.ds(0, ROWS)],
                ss.at[b, d], rs.at[b, d], (d * HIGH + zl, t),
            )
            if which == "in":
                copy.wait_recv()
            else:
                copy.wait_send()
            return carry

        lax.fori_loop(1, PLANE, one, 0)
        if which == "in":
            pltpu.make_async_copy(
                src.at[b, p, pl.ds(0, ROWS)], dst.at[b, p, pl.ds(0, ROWS)], ls.at[b]
            ).wait()

    def route(b):
        ids = (lax.broadcasted_iota(jnp.int32, (PLANE, tokens), 0) * HIGH + zl).astype(F32)
        first = lax.broadcasted_iota(jnp.int32, (tokens, tokens), 0)
        second = lax.broadcasted_iota(jnp.int32, (tokens, tokens), 1)
        ahead = jnp.where(first < second, 1.0, 0.0).astype(BF16)
        targets, gates = [], []
        for i in range(LINE):
            info = rg[b, i]
            named = jnp.zeros((PLANE, tokens), F32)
            gate = jnp.zeros((PLANE, tokens), F32)
            for k in range(8):
                same = info[k:k + 1, :] == ids
                named = named + jnp.where(same, 1.0, 0.0)
                gate = gate + jnp.where(same, info[8 + k:9 + k, :], 0.0)
            rank = jnp.dot(named.astype(BF16), ahead, preferred_element_type=F32)
            targets.append(jnp.where(named > 0.5, rank * LINE + i, -1.0))
            gates.append(gate)
        tgt[b] = jnp.concatenate(targets, axis=1)
        gat[b] = jnp.concatenate(gates, axis=1)

    places = lax.broadcasted_iota(jnp.int32, (PAD, LINE * tokens), 0).astype(F32)

    def dispatch(b):
        for i in range(1, LINE):
            line_x(b, i).wait_recv()
            line_r(b, i).wait_recv()
        route(b)
        for d in range(PLANE):
            pick[d] = jnp.where(tgt[b, d:d + 1, :] == places, 1.0, 0.0).astype(BF16)
        for k in ORDER:
            q = (px + k) % WIDE
            rows = pick[pl.ds(q * WIDE, WIDE)].reshape(WIDE * PAD, LINE * tokens)
            block = jnp.dot(
                rows, xg[b].reshape(LINE * tokens, features), preferred_element_type=F32
            ).astype(BF16)
            outg[b, pl.ds(q * WIDE, WIDE)] = block.reshape(WIDE, PAD, features)
            group_send(b, q, outg, recv, a_s, a_r, a_l)

    def experts_on(b, v, k):
        q = (px + k) % WIDE
        rows = recv[b, pl.ds(q * WIDE, WIDE)].reshape(WIDE * PAD, features)
        gate_act = jnp.dot(rows, wg[v].reshape(features, inner), preferred_element_type=F32)
        up_act = jnp.dot(rows, wu[v].reshape(features, inner), preferred_element_type=F32)
        hidden = (gate_act / (1.0 + jnp.exp(-gate_act)) * up_act).astype(BF16)
        result = lax.dot_general(
            hidden, wd[v].reshape(features, inner), (((1,), (1,)), ((), ())),
            preferred_element_type=F32,
        ).astype(BF16)
        res[b, pl.ds(q * WIDE, WIDE)] = result.reshape(WIDE, PAD, features)

    def results_send(b, k):
        group_send(b, (px + k) % WIDE, res, back, b_s, b_r, b_l)

    def combine(b):
        for d in range(PLANE):
            pick[d] = jnp.where(
                tgt[b, d:d + 1, :] == places, gat[b, d:d + 1, :], 0.0
            ).astype(BF16)
        mixer = pick[...].reshape(PLANE * PAD, LINE * tokens)
        total = lax.dot_general(
            mixer, back[b].reshape(PLANE * PAD, features), (((0,), (0,)), ((), ())),
            preferred_element_type=F32,
        ).astype(BF16)
        part[b] = total.reshape(LINE, tokens, features)
        for i in range(1, LINE):
            part_out(b, i).start()

    def finish(b, out):
        total = part[b, 0].astype(F32)
        for i in range(1, LINE):
            part_out(b, i).wait_recv()
            total = total + precv[b, i].astype(F32)
        out[...] = total

    dispatch(0)
    tick(1)
    dispatch(1)
    for piece in (2, 3, 4, 5, REST, 6):
        tick(piece)
    edge_arrive(1)
    tick(7)
    edge_arrive(3)
    tick(8)

    block_wait(0, outg, recv, a_s, a_r, a_l, "in")
    for m in range(3):
        own_in(m).wait_recv()
        for piece in (4, 8):
            for way in range(2):
                sib(way, piece, m).wait_recv()
    for k in ORDER:
        experts_on(0, zl, k)
    tick(9)
    edge_arrive(5, REST, 7, 9)
    for dx, dy in FAR_FIRST:
        block_send(0, (px + dx) % WIDE * WIDE + (py + dy) % WIDE, res, back, b_s, b_r, b_l)
    block_wait(1, outg, recv, a_s, a_r, a_l, "in")
    for m in range(3):
        for piece in SHARED:
            if piece not in (4, 8):
                for way in range(2):
                    sib(way, piece, m).wait_recv()

    @pl.when(on_edge)
    def _():
        for m in range(3):
            for piece in EDGES:
                esib(piece, m).wait_recv()

    wanted = tnew[e]
    keeps = wanted == told[e]
    lower = wanted == told[(e + experts - 1) % experts]
    bottom = 1 - (zl + HIGH - 1) // HIGH
    column = jnp.where(
        keeps, zl, jnp.where(lower, zl - 1 + bottom * (HIGH + 1), zl + 1)
    )
    for k in ORDER:
        experts_on(1, column, k)
        results_send(1, k)
    block_wait(0, res, back, b_s, b_r, b_l, "in")
    combine(0)
    block_wait(1, res, back, b_s, b_r, b_l, "in")
    combine(1)
    finish(0, o1)
    finish(1, o2)

    for m in range(3):
        own(m).wait_send()
        for way in range(2):
            for piece in range(1, REST + 1):
                ring(way, piece, m).wait_send()
            for piece in SHARED:
                sib(way, piece, m).wait_send()

    @pl.when(on_edge)
    def _():
        for m in range(3):
            for piece in EDGES:
                edge(piece, m).wait_send()
                esib(piece, m).wait_send()

    for b in range(2):
        for i in range(1, LINE):
            line_x(b, i).wait_send()
            line_r(b, i).wait_send()
            part_out(b, i).wait_send()
        block_wait(b, outg, recv, a_s, a_r, a_l, "out")
        block_wait(b, res, back, b_s, b_r, b_l, "out")


def local(
    batch_one, batch_two, norm_gain, slots_one, slots_two, gates_one, gates_two,
    table_old, table_new, gate_old, up_old, down_old,
):
    tokens, features = batch_one.shape
    shard, inner = gate_old.shape[1:]
    vmem = pl.BlockSpec(memory_space=pltpu.VMEM)
    smem = pl.BlockSpec(memory_space=pltpu.SMEM)
    dma = pltpu.SemaphoreType.DMA
    full = pltpu.VMEM((HIGH + 1, HIGH, 2, shard, inner), BF16)
    blocks = pltpu.VMEM((2, PLANE, PAD, features), BF16)
    line = pltpu.VMEM((2, LINE, tokens, features), BF16)
    one, two = pl.pallas_call(
        body,
        out_shape=[jax.ShapeDtypeStruct((tokens, features), F32)] * 2,
        in_specs=[vmem] * 7 + [smem] * 2 + [vmem] * 3,
        out_specs=[vmem] * 2,
        scratch_shapes=[
            full, full, full,
            line, pltpu.VMEM((2, LINE, 16, tokens), F32),
            blocks, blocks, blocks, blocks,
            pltpu.VMEM((PLANE, PAD, LINE * tokens), BF16),
            line, line,
            pltpu.VMEM((2, PLANE, LINE * tokens), F32), pltpu.VMEM((2, PLANE, LINE * tokens), F32),
            dma((2, REST, 3)), dma((2, REST, 3)), dma((3,)), dma((3,)),
            dma((2, len(SHARED), 3)), dma((2, len(SHARED), 3)),
            dma((6, 3)), dma((6, 3)), dma((6, 3)), dma((6, 3)),
            dma((2, LINE)), dma((2, LINE)), dma((2, LINE)), dma((2, LINE)),
            dma((2, PLANE)), dma((2, PLANE)), dma((2,)),
            dma((2, PLANE)), dma((2, PLANE)), dma((2,)),
            dma((2, LINE)), dma((2, LINE)),
        ],
        compiler_params=pltpu.CompilerParams(
            collective_id=0, has_side_effects=True, vmem_limit_bytes=60 * 1024 * 1024
        ),
    )(
        batch_one, batch_two, norm_gain, slots_one.T, slots_two.T, gates_one.T, gates_two.T,
        table_old, table_new, gate_old[0], up_old[0], down_old[0].T,
    )
    return one.astype(BF16), two.astype(BF16)


def solution(mesh):
    rows = P(("expert", "tensor"), None)
    in_specs = (
        rows, rows, P(), rows, rows, rows, rows, P(), P(),
        P("expert", "tensor", None), P("expert", "tensor", None), P("expert", None, "tensor"),
    )
    return jax.shard_map(
        local, mesh=mesh, in_specs=in_specs, out_specs=(rows, rows), check_vma=False
    )
```

```python
import functools

import jax
import jax.numpy as jnp
from jax import lax
from jax.experimental import pallas as pl
from jax.experimental.pallas import tpu as pltpu
from jax.sharding import PartitionSpec as P

EPS = 1e-05
MESH = pl.DeviceIdType.MESH
BF16 = jnp.bfloat16
F32 = jnp.float32

LINE = 4
DEPTH = 16
PLANE = 16
HIGH = 4
WIDE = 4
ROWS = 40
PAD = 48
WHOLE = 4
HOPS = 9
REST = 10
SHARED = (1, 3, 4, 5, 7, 8, 9, REST)
EDGES = (1, 3, 5, 7, 9, REST)
ORDER = (2, 1, 3, 0)
FAR_FIRST = sorted(
    ((dx, dy) for dx in range(WIDE) for dy in range(WIDE)),
    key=lambda d: (-min(d[0], WIDE - d[0]) - min(d[1], WIDE - d[1]), d),
)


def body(
    x1, x2, gain, s1, s2, g1, g2, told, tnew, gate_in, up_in, down_in,
    out,
    wg, wu, wd, xg, rg, outg, recv, res, back, pick, part, precv, tgt, gat,
    ring_s, ring_r, own_s, own_r, sib_s, sib_r, edge_s, edge_r, esib_s, esib_r,
    zx_s, zx_r, zr_s, zr_r, a_s, a_r, a_l, b_s, b_r, b_l, p_s, p_r,
):
    e = lax.axis_index("expert")
    t = lax.axis_index("tensor")
    experts = lax.axis_size("expert")
    zl = e % HIGH
    p = e // HIGH
    px = p // WIDE
    py = p % WIDE
    zh = t // 2
    c = t % 2
    z = zh * HIGH + zl
    top = (zl + 1) // HIGH
    on_edge = zl % (HIGH - 1) == 0
    skip = 2 * (1 - 2 * (z % 2))
    sibling = (e, zh * 2 + (1 - c))
    weights = (wg, wu, wd)
    shards = (gate_in, up_in, down_in)
    tokens, features = x1.shape
    shard, inner = gate_in.shape

    def along(distance):
        other = (z + distance + 2 * DEPTH) % DEPTH
        return (p * HIGH + other % HIGH, (other // HIGH) * 2 + c)

    def remote(src, dst, ss, rs, device):
        return pltpu.make_async_remote_copy(
            src_ref=src, dst_ref=dst, send_sem=ss, recv_sem=rs,
            device_id=device, device_id_type=MESH,
        )

    barrier = pltpu.get_barrier_semaphore()

    def greet(device):
        pl.semaphore_signal(barrier, inc=1, device_id=device, device_id_type=MESH)

    for device in (along(1), along(-1), along(2), along(-2), sibling):
        greet(device)

    def greet_plane(o, carry):
        greet((((p + o) % PLANE) * HIGH + zl, t))
        return carry

    lax.fori_loop(1, PLANE, greet_plane, 0)
    pl.semaphore_wait(barrier, 5 + PLANE - 1)

    def spot(m, column, owner, piece, way):
        place = weights[m].at[column, owner // HIGH, c]
        if piece <= WHOLE:
            return place
        half = 1 - way if piece == REST else way
        return place.at[pl.ds(pl.multiple_of(half * (shard // 2), shard // 2), shard // 2)]

    def source(piece, way, back_off=0):
        distance = (WHOLE + 1 if piece == REST else piece) - back_off
        return (z - (1 - 2 * way) * distance + 2 * DEPTH) % DEPTH

    def ring(way, piece, m):
        owner = source(piece, way, 1)
        place = spot(m, owner % HIGH, owner, piece, way)
        return remote(
            shards[m] if piece == 1 else place, place,
            ring_s.at[way, piece - 1, m], ring_r.at[way, piece - 1, m], along(1 - 2 * way),
        )

    def ring_in(way, piece, m):
        owner = source(piece, way)
        place = spot(m, owner % HIGH, owner, piece, way)
        return remote(
            place, place, ring_s.at[way, piece - 1, m], ring_r.at[way, piece - 1, m],
            along(1 - 2 * way),
        )

    def own(m):
        return remote(shards[m], weights[m].at[zl, zh, c], own_s.at[m], own_r.at[m], sibling)

    def own_in(m):
        return remote(
            shards[m], weights[m].at[zl, zh, 1 - c], own_s.at[m], own_r.at[m], sibling
        )

    def sib(way, piece, m):
        owner = source(piece, way)
        place = spot(m, owner % HIGH, owner, piece, way)
        k = SHARED.index(piece)
        return remote(place, place, sib_s.at[way, k, m], sib_r.at[way, k, m], sibling)

    def edge_way(piece):
        return 1 - top if piece % 4 == 3 else top

    def edge(piece, m):
        way = edge_way(piece)
        owner = source(piece, way)
        src = spot(m, owner % HIGH, owner, piece, way)
        dst = spot(m, HIGH, owner, piece, way)
        column = (e + HIGH * (1 - 2 * top) + experts) % experts
        k = EDGES.index(piece)
        return remote(src, dst, edge_s.at[k, m], edge_r.at[k, m], (column, t))

    def esib(piece, m):
        way = edge_way(piece)
        owner = source(piece, way)
        place = spot(m, HIGH, owner, piece, way)
        k = EDGES.index(piece)
        return remote(place, place, esib_s.at[k, m], esib_r.at[k, m], sibling)

    def edge_arrive(*pieces):
        @pl.when(on_edge)
        def _():
            for piece in pieces:
                for m in range(3):
                    edge(piece, m).wait_recv()
                    esib(piece, m).start()

    def tick(piece):
        for m in range(3):
            for way in range(2):
                ring_in(way, piece, m).wait_recv()
                if piece < HOPS:
                    ring(way, piece + 1, m).start()
        if piece == WHOLE:
            for m in range(3):
                for way in range(2):
                    ring(way, REST, m).start()
        if piece in EDGES:
            @pl.when(on_edge)
            def _():
                for m in range(3):
                    edge(piece, m).start()
        if piece in SHARED:
            for m in range(3):
                for way in range(2):
                    sib(way, piece, m).start()

    for m in range(3):
        for way in range(2):
            ring(way, 1, m).start()
    for m in range(3):
        own(m).start()

    targets_of = (None, along(1), along(-1), along(skip))
    sources_of = (None, along(-1), along(1), along(-skip))

    def line_x(b, i):
        return remote(xg.at[b, 0], xg.at[b, i], zx_s.at[b, i], zx_r.at[b, i], targets_of[i])

    def line_r(b, i):
        return remote(rg.at[b, 0], rg.at[b, i], zr_s.at[b, i], zr_r.at[b, i], targets_of[i])

    scale = gain[...].astype(F32)
    for b, (x, slots, gates) in enumerate(((x1, s1, g1), (x2, s2, g2))):
        values = x[...].astype(F32)
        square = jnp.mean(values * values, axis=-1, keepdims=True)
        xg[b, 0] = (values * lax.rsqrt(square + EPS) * scale).astype(BF16)
        rg[b, 0, 0:8] = slots[...].astype(F32)
        rg[b, 0, 8:16] = gates[...]
        for i in range(1, LINE):
            line_x(b, i).start()
            line_r(b, i).start()

    for w, mine in zip(weights, shards):
        w[zl, zh, c] = mine[...]

    blank = jnp.zeros((PLANE, PAD - ROWS, features), BF16)
    for b in range(2):
        recv[b, :, ROWS:PAD, :] = blank
        back[b, :, ROWS:PAD, :] = blank

    def rows_of(ref, b, d, cut):
        if cut == 0:
            return ref.at[b, d, pl.ds(0, ROWS)]
        return ref.at[b, d, pl.ds(0, ROWS), pl.ds((cut - 1) * (features // 2), features // 2)]

    def block_send(b, d, src, dst, ss, rs, ls, cut=0):
        k = b + max(cut - 1, 0)

        @pl.when(d != p)
        def _():
            remote(
                rows_of(src, b, d, cut), rows_of(dst, b, p, cut),
                ss.at[k, d], rs.at[k, p], (d * HIGH + zl, t),
            ).start()

        @pl.when(d == p)
        def _():
            pltpu.make_async_copy(
                rows_of(src, b, d, cut), rows_of(dst, b, p, cut), ls.at[k]
            ).start()

    def group_send(b, q, src, dst, ss, rs, ls):
        for k in ORDER:
            block_send(b, q * WIDE + (py + k) % WIDE, src, dst, ss, rs, ls)

    def block_wait(b, src, dst, ss, rs, ls, which, cut=0):
        k = b + max(cut - 1, 0)

        def one(o, carry):
            d = (p + o) % PLANE
            copy = remote(
                rows_of(src, b, d, cut), rows_of(dst, b, d, cut),
                ss.at[k, d], rs.at[k, d], (d * HIGH + zl, t),
            )
            if which == "in":
                copy.wait_recv()
            else:
                copy.wait_send()
            return carry

        lax.fori_loop(1, PLANE, one, 0)
        if which == "in":
            pltpu.make_async_copy(
                rows_of(src, b, p, cut), rows_of(dst, b, p, cut), ls.at[k]
            ).wait()

    def route(b):
        ids = (lax.broadcasted_iota(jnp.int32, (PLANE, tokens), 0) * HIGH + zl).astype(F32)
        first = lax.broadcasted_iota(jnp.int32, (tokens, tokens), 0)
        second = lax.broadcasted_iota(jnp.int32, (tokens, tokens), 1)
        ahead = jnp.where(first < second, 1.0, 0.0).astype(BF16)
        targets, gates = [], []
        for i in range(LINE):
            info = rg[b, i]
            named = jnp.zeros((PLANE, tokens), F32)
            gate = jnp.zeros((PLANE, tokens), F32)
            for k in range(8):
                same = info[k:k + 1, :] == ids
                named = named + jnp.where(same, 1.0, 0.0)
                gate = gate + jnp.where(same, info[8 + k:9 + k, :], 0.0)
            rank = jnp.dot(named.astype(BF16), ahead, preferred_element_type=F32)
            targets.append(jnp.where(named > 0.5, rank * LINE + i, -1.0))
            gates.append(gate)
        tgt[b] = jnp.concatenate(targets, axis=1)
        gat[b] = jnp.concatenate(gates, axis=1)

    places = lax.broadcasted_iota(jnp.int32, (PAD, LINE * tokens), 0).astype(F32)

    def dispatch(b):
        for i in range(1, LINE):
            line_x(b, i).wait_recv()
            line_r(b, i).wait_recv()
        route(b)
        for d in range(PLANE):
            pick[d] = jnp.where(tgt[b, d:d + 1, :] == places, 1.0, 0.0).astype(BF16)
        for k in ORDER:
            q = (px + k) % WIDE
            rows = pick[pl.ds(q * WIDE, WIDE)].reshape(WIDE * PAD, LINE * tokens)
            block = jnp.dot(
                rows, xg[b].reshape(LINE * tokens, features), preferred_element_type=F32
            ).astype(BF16)
            outg[b, pl.ds(q * WIDE, WIDE)] = block.reshape(WIDE, PAD, features)
            group_send(b, q, outg, recv, a_s, a_r, a_l)

    def experts_on(b, v, k):
        q = (px + k) % WIDE
        rows = recv[b, pl.ds(q * WIDE, WIDE)].reshape(WIDE * PAD, features)
        gate_act = jnp.dot(rows, wg[v].reshape(features, inner), preferred_element_type=F32)
        up_act = jnp.dot(rows, wu[v].reshape(features, inner), preferred_element_type=F32)
        hidden = (gate_act / (1.0 + jnp.exp(-gate_act)) * up_act).astype(BF16)
        result = lax.dot_general(
            hidden, wd[v].reshape(features, inner), (((1,), (1,)), ((), ())),
            preferred_element_type=F32,
        ).astype(BF16)
        res[b, pl.ds(q * WIDE, WIDE)] = result.reshape(WIDE, PAD, features)

    def results_send(b, cut):
        for dx, dy in FAR_FIRST:
            d = (px + dx) % WIDE * WIDE + (py + dy) % WIDE
            block_send(b, d, res, back, b_s, b_r, b_l, cut)

    def lanes(cut):
        if cut == 0:
            return pl.ds(0, features)
        return pl.ds((cut - 1) * (features // 2), features // 2)

    def part_out(b, i, cut):
        k = b + max(cut - 1, 0)
        return remote(
            part.at[b, i, :, lanes(cut)], precv.at[b, i, :, lanes(cut)],
            p_s.at[k, i], p_r.at[k, i], sources_of[i],
        )

    def weigh(b):
        for d in range(PLANE):
            pick[d] = jnp.where(
                tgt[b, d:d + 1, :] == places, gat[b, d:d + 1, :], 0.0
            ).astype(BF16)

    def combine(b, cut):
        mixer = pick[...].reshape(PLANE * PAD, LINE * tokens)
        results = back[b, :, :, lanes(cut)]
        width = results.shape[2]
        total = lax.dot_general(
            mixer, results.reshape(PLANE * PAD, width), (((0,), (0,)), ((), ())),
            preferred_element_type=F32,
        ).astype(BF16)
        part[b, :, :, lanes(cut)] = total.reshape(LINE, tokens, width)
        for i in range(1, LINE):
            part_out(b, i, cut).start()

    def finish(b, cut):
        total = part[b, 0, :, lanes(cut)].astype(F32)
        for i in range(1, LINE):
            part_out(b, i, cut).wait_recv()
            total = total + precv[b, i, :, lanes(cut)].astype(F32)
        out[b, :, lanes(cut)] = total

    dispatch(0)
    tick(1)
    dispatch(1)
    for piece in (2, 3, 4, 5, REST, 6):
        tick(piece)
    edge_arrive(1)
    tick(7)
    edge_arrive(3)
    tick(8)

    block_wait(0, outg, recv, a_s, a_r, a_l, "in")
    for m in range(3):
        own_in(m).wait_recv()
        for piece in (4, 8):
            for way in range(2):
                sib(way, piece, m).wait_recv()
    for k in ORDER:
        experts_on(0, zl, k)
    tick(9)
    edge_arrive(5, REST, 7, 9)
    results_send(0, 0)
    block_wait(1, outg, recv, a_s, a_r, a_l, "in")
    for m in range(3):
        for piece in SHARED:
            if piece not in (4, 8):
                for way in range(2):
                    sib(way, piece, m).wait_recv()

    @pl.when(on_edge)
    def _():
        for m in range(3):
            for piece in EDGES:
                esib(piece, m).wait_recv()

    wanted = tnew[e]
    keeps = wanted == told[e]
    lower = wanted == told[(e + experts - 1) % experts]
    bottom = 1 - (zl + HIGH - 1) // HIGH
    column = jnp.where(
        keeps, zl, jnp.where(lower, zl - 1 + bottom * (HIGH + 1), zl + 1)
    )
    for k in ORDER:
        experts_on(1, column, k)
    for cut in (1, 2):
        results_send(1, cut)
    weigh(0)
    block_wait(0, res, back, b_s, b_r, b_l, "in")
    combine(0, 0)
    weigh(1)
    for cut in (1, 2):
        block_wait(1, res, back, b_s, b_r, b_l, "in", cut)
        combine(1, cut)
    finish(0, 0)
    for cut in (1, 2):
        finish(1, cut)

    for m in range(3):
        own(m).wait_send()
        for way in range(2):
            for piece in range(1, REST + 1):
                ring(way, piece, m).wait_send()
            for piece in SHARED:
                sib(way, piece, m).wait_send()

    @pl.when(on_edge)
    def _():
        for m in range(3):
            for piece in EDGES:
                edge(piece, m).wait_send()
                esib(piece, m).wait_send()

    for b in range(2):
        for i in range(1, LINE):
            line_x(b, i).wait_send()
            line_r(b, i).wait_send()
        block_wait(b, outg, recv, a_s, a_r, a_l, "out")
    for b, cut in ((0, 0), (1, 1), (1, 2)):
        for i in range(1, LINE):
            part_out(b, i, cut).wait_send()
        block_wait(b, res, back, b_s, b_r, b_l, "out", cut)


def local(
    batch_one, batch_two, norm_gain, slots_one, slots_two, gates_one, gates_two,
    table_old, table_new, gate_old, up_old, down_old,
):
    tokens, features = batch_one.shape
    shard, inner = gate_old.shape[1:]
    vmem = pl.BlockSpec(memory_space=pltpu.VMEM)
    smem = pl.BlockSpec(memory_space=pltpu.SMEM)
    dma = pltpu.SemaphoreType.DMA
    full = pltpu.VMEM((HIGH + 1, HIGH, 2, shard, inner), BF16)
    blocks = pltpu.VMEM((2, PLANE, PAD, features), BF16)
    line = pltpu.VMEM((2, LINE, tokens, features), BF16)
    mixed = pl.pallas_call(
        body,
        out_shape=jax.ShapeDtypeStruct((2, tokens, features), F32),
        in_specs=[vmem] * 7 + [smem] * 2 + [vmem] * 3,
        out_specs=vmem,
        scratch_shapes=[
            full, full, full,
            line, pltpu.VMEM((2, LINE, 16, tokens), F32),
            blocks, blocks, blocks, blocks,
            pltpu.VMEM((PLANE, PAD, LINE * tokens), BF16),
            line, line,
            pltpu.VMEM((2, PLANE, LINE * tokens), F32), pltpu.VMEM((2, PLANE, LINE * tokens), F32),
            dma((2, REST, 3)), dma((2, REST, 3)), dma((3,)), dma((3,)),
            dma((2, len(SHARED), 3)), dma((2, len(SHARED), 3)),
            dma((6, 3)), dma((6, 3)), dma((6, 3)), dma((6, 3)),
            dma((2, LINE)), dma((2, LINE)), dma((2, LINE)), dma((2, LINE)),
            dma((2, PLANE)), dma((2, PLANE)), dma((2,)),
            dma((3, PLANE)), dma((3, PLANE)), dma((3,)),
            dma((3, LINE)), dma((3, LINE)),
        ],
        compiler_params=pltpu.CompilerParams(
            collective_id=0, has_side_effects=True, vmem_limit_bytes=60 * 1024 * 1024
        ),
    )(
        batch_one, batch_two, norm_gain, slots_one.T, slots_two.T, gates_one.T, gates_two.T,
        table_old, table_new, gate_old[0], up_old[0], down_old[0].T,
    )
    return mixed[0].astype(BF16), mixed[1].astype(BF16)


def solution(mesh):
    rows = P(("expert", "tensor"), None)
    in_specs = (
        rows, rows, P(), rows, rows, rows, rows, P(), P(),
        P("expert", "tensor", None), P("expert", "tensor", None), P("expert", None, "tensor"),
    )
    return jax.shard_map(
        local, mesh=mesh, in_specs=in_specs, out_specs=(rows, rows), check_vma=False
    )
```

```python
import functools

import jax
import jax.numpy as jnp
from jax import lax
from jax.experimental import pallas as pl
from jax.experimental.pallas import tpu as pltpu
from jax.sharding import PartitionSpec as P

EPS = 1e-05
MESH = pl.DeviceIdType.MESH
BF16 = jnp.bfloat16
F32 = jnp.float32

LINE = 4
DEPTH = 16
PLANE = 16
HIGH = 4
WIDE = 4
ROWS = 40
PAD = 48
WHOLE = 4
HOPS = 9
REST = 10
SHARED = (1, 3, 4, 5, 7, 8, 9, REST)
EDGES = (1, 3, 5, 7, 9, REST)
ORDER = (2, 1, 3, 0)
FAR_FIRST = sorted(
    ((dx, dy) for dx in range(WIDE) for dy in range(WIDE)),
    key=lambda d: (-min(d[0], WIDE - d[0]) - min(d[1], WIDE - d[1]), d),
)


def body(
    x1, x2, gain, s1, s2, g1, g2, told, tnew, gate_in, up_in, down_in,
    out,
    wg, wu, wd, xg, rg, outg, recv, res, back, pick, part, precv, tgt, gat,
    ring_s, ring_r, own_s, own_r, sib_s, sib_r, edge_s, edge_r, esib_s, esib_r,
    zx_s, zx_r, zr_s, zr_r, a_s, a_r, a_l, b_s, b_r, b_l, p_s, p_r,
):
    e = lax.axis_index("expert")
    t = lax.axis_index("tensor")
    experts = lax.axis_size("expert")
    zl = e % HIGH
    p = e // HIGH
    px = p // WIDE
    py = p % WIDE
    zh = t // 2
    c = t % 2
    z = zh * HIGH + zl
    top = (zl + 1) // HIGH
    on_edge = zl % (HIGH - 1) == 0
    skip = 2 * (1 - 2 * (z % 2))
    sibling = (e, zh * 2 + (1 - c))
    weights = (wg, wu, wd)
    shards = (gate_in, up_in, down_in)
    tokens, features = x1.shape
    shard, inner = gate_in.shape

    def along(distance):
        other = (z + distance + 2 * DEPTH) % DEPTH
        return (p * HIGH + other % HIGH, (other // HIGH) * 2 + c)

    def remote(src, dst, ss, rs, device):
        return pltpu.make_async_remote_copy(
            src_ref=src, dst_ref=dst, send_sem=ss, recv_sem=rs,
            device_id=device, device_id_type=MESH,
        )

    barrier = pltpu.get_barrier_semaphore()

    def greet(device):
        pl.semaphore_signal(barrier, inc=1, device_id=device, device_id_type=MESH)

    for device in (along(1), along(-1), along(2), along(-2), sibling):
        greet(device)

    def greet_plane(o, carry):
        greet((((p + o) % PLANE) * HIGH + zl, t))
        return carry

    lax.fori_loop(1, PLANE, greet_plane, 0)
    pl.semaphore_wait(barrier, 5 + PLANE - 1)

    def spot(m, column, owner, piece, way):
        place = weights[m].at[column, owner // HIGH, c]
        if piece <= WHOLE:
            return place
        half = 1 - way if piece == REST else way
        return place.at[pl.ds(pl.multiple_of(half * (shard // 2), shard // 2), shard // 2)]

    def source(piece, way, back_off=0):
        distance = (WHOLE + 1 if piece == REST else piece) - back_off
        return (z - (1 - 2 * way) * distance + 2 * DEPTH) % DEPTH

    def ring(way, piece, m):
        owner = source(piece, way, 1)
        place = spot(m, owner % HIGH, owner, piece, way)
        return remote(
            shards[m] if piece == 1 else place, place,
            ring_s.at[way, piece - 1, m], ring_r.at[way, piece - 1, m], along(1 - 2 * way),
        )

    def ring_in(way, piece, m):
        owner = source(piece, way)
        place = spot(m, owner % HIGH, owner, piece, way)
        return remote(
            place, place, ring_s.at[way, piece - 1, m], ring_r.at[way, piece - 1, m],
            along(1 - 2 * way),
        )

    def own(m):
        return remote(shards[m], weights[m].at[zl, zh, c], own_s.at[m], own_r.at[m], sibling)

    def own_in(m):
        return remote(
            shards[m], weights[m].at[zl, zh, 1 - c], own_s.at[m], own_r.at[m], sibling
        )

    def sib(way, piece, m):
        owner = source(piece, way)
        place = spot(m, owner % HIGH, owner, piece, way)
        k = SHARED.index(piece)
        return remote(place, place, sib_s.at[way, k, m], sib_r.at[way, k, m], sibling)

    def edge_way(piece):
        return 1 - top if piece % 4 == 3 else top

    def edge(piece, m):
        way = edge_way(piece)
        owner = source(piece, way)
        src = spot(m, owner % HIGH, owner, piece, way)
        dst = spot(m, HIGH, owner, piece, way)
        column = (e + HIGH * (1 - 2 * top) + experts) % experts
        k = EDGES.index(piece)
        return remote(src, dst, edge_s.at[k, m], edge_r.at[k, m], (column, t))

    def esib(piece, m):
        way = edge_way(piece)
        owner = source(piece, way)
        place = spot(m, HIGH, owner, piece, way)
        k = EDGES.index(piece)
        return remote(place, place, esib_s.at[k, m], esib_r.at[k, m], sibling)

    def edge_arrive(*pieces):
        @pl.when(on_edge)
        def _():
            for piece in pieces:
                for m in range(3):
                    edge(piece, m).wait_recv()
                    esib(piece, m).start()

    def tick(piece):
        for m in range(3):
            for way in range(2):
                ring_in(way, piece, m).wait_recv()
                if piece < HOPS:
                    ring(way, piece + 1, m).start()
        if piece == WHOLE:
            for m in range(3):
                for way in range(2):
                    ring(way, REST, m).start()
        if piece in EDGES:
            @pl.when(on_edge)
            def _():
                for m in range(3):
                    edge(piece, m).start()
        if piece in SHARED:
            for m in range(3):
                for way in range(2):
                    sib(way, piece, m).start()

    for m in range(3):
        for way in range(2):
            ring(way, 1, m).start()
    for m in range(3):
        own(m).start()

    targets_of = (None, along(1), along(-1), along(skip))
    sources_of = (None, along(-1), along(1), along(-skip))

    def line_x(b, i):
        return remote(xg.at[b, 0], xg.at[b, i], zx_s.at[b, i], zx_r.at[b, i], targets_of[i])

    def line_r(b, i):
        return remote(rg.at[b, 0], rg.at[b, i], zr_s.at[b, i], zr_r.at[b, i], targets_of[i])

    scale = gain[...].astype(F32)
    for b, (x, slots, gates) in enumerate(((x1, s1, g1), (x2, s2, g2))):
        values = x[...].astype(F32)
        square = jnp.mean(values * values, axis=-1, keepdims=True)
        xg[b, 0] = (values * lax.rsqrt(square + EPS) * scale).astype(BF16)
        rg[b, 0, 0:8] = slots[...].astype(F32)
        rg[b, 0, 8:16] = gates[...]
        for i in range(1, LINE):
            line_x(b, i).start()
            line_r(b, i).start()

    for w, mine in zip(weights, shards):
        w[zl, zh, c] = mine[...]

    blank = jnp.zeros((PLANE, PAD - ROWS, features), BF16)
    for b in range(2):
        recv[b, :, ROWS:PAD, :] = blank
        back[b, :, ROWS:PAD, :] = blank

    def rows_of(ref, b, d, cut):
        if cut == 0:
            return ref.at[b, d, pl.ds(0, ROWS)]
        return ref.at[b, d, pl.ds(0, ROWS), pl.ds((cut - 1) * (features // 2), features // 2)]

    def block_send(b, d, src, dst, ss, rs, ls, cut=0):
        k = b + max(cut - 1, 0)

        @pl.when(d != p)
        def _():
            remote(
                rows_of(src, b, d, cut), rows_of(dst, b, p, cut),
                ss.at[k, d], rs.at[k, p], (d * HIGH + zl, t),
            ).start()

        @pl.when(d == p)
        def _():
            pltpu.make_async_copy(
                rows_of(src, b, d, cut), rows_of(dst, b, p, cut), ls.at[k]
            ).start()

    def group_send(b, q, src, dst, ss, rs, ls):
        for k in ORDER:
            block_send(b, q * WIDE + (py + k) % WIDE, src, dst, ss, rs, ls)

    def block_wait(b, src, dst, ss, rs, ls, which, cut=0):
        k = b + max(cut - 1, 0)

        def one(o, carry):
            d = (p + o) % PLANE
            copy = remote(
                rows_of(src, b, d, cut), rows_of(dst, b, d, cut),
                ss.at[k, d], rs.at[k, d], (d * HIGH + zl, t),
            )
            if which == "in":
                copy.wait_recv()
            else:
                copy.wait_send()
            return carry

        lax.fori_loop(1, PLANE, one, 0)
        if which == "in":
            pltpu.make_async_copy(
                rows_of(src, b, p, cut), rows_of(dst, b, p, cut), ls.at[k]
            ).wait()

    def route(b):
        ids = (lax.broadcasted_iota(jnp.int32, (PLANE, tokens), 0) * HIGH + zl).astype(F32)
        first = lax.broadcasted_iota(jnp.int32, (tokens, tokens), 0)
        second = lax.broadcasted_iota(jnp.int32, (tokens, tokens), 1)
        ahead = jnp.where(first < second, 1.0, 0.0).astype(BF16)
        targets, gates = [], []
        for i in range(LINE):
            info = rg[b, i]
            named = jnp.zeros((PLANE, tokens), F32)
            gate = jnp.zeros((PLANE, tokens), F32)
            for k in range(8):
                same = info[k:k + 1, :] == ids
                named = named + jnp.where(same, 1.0, 0.0)
                gate = gate + jnp.where(same, info[8 + k:9 + k, :], 0.0)
            rank = jnp.dot(named.astype(BF16), ahead, preferred_element_type=F32)
            targets.append(jnp.where(named > 0.5, rank * LINE + i, -1.0))
            gates.append(gate)
        tgt[b] = jnp.concatenate(targets, axis=1)
        gat[b] = jnp.concatenate(gates, axis=1)

    places = lax.broadcasted_iota(jnp.int32, (PAD, LINE * tokens), 0).astype(F32)

    def dispatch(b):
        for i in range(1, LINE):
            line_x(b, i).wait_recv()
            line_r(b, i).wait_recv()
        route(b)
        for d in range(PLANE):
            pick[d] = jnp.where(tgt[b, d:d + 1, :] == places, 1.0, 0.0).astype(BF16)
        for k in ORDER:
            q = (px + k) % WIDE
            rows = pick[pl.ds(q * WIDE, WIDE)].reshape(WIDE * PAD, LINE * tokens)
            block = jnp.dot(
                rows, xg[b].reshape(LINE * tokens, features), preferred_element_type=F32
            ).astype(BF16)
            outg[b, pl.ds(q * WIDE, WIDE)] = block.reshape(WIDE, PAD, features)
            group_send(b, q, outg, recv, a_s, a_r, a_l)

    def experts_on(b, v, k):
        q = (px + k) % WIDE
        rows = recv[b, pl.ds(q * WIDE, WIDE)].reshape(WIDE * PAD, features)
        gate_act = jnp.dot(rows, wg[v].reshape(features, inner), preferred_element_type=F32)
        up_act = jnp.dot(rows, wu[v].reshape(features, inner), preferred_element_type=F32)
        hidden = (gate_act / (1.0 + jnp.exp(-gate_act)) * up_act).astype(BF16)
        result = lax.dot_general(
            hidden, wd[v].reshape(features, inner), (((1,), (1,)), ((), ())),
            preferred_element_type=F32,
        ).astype(BF16)
        res[b, pl.ds(q * WIDE, WIDE)] = result.reshape(WIDE, PAD, features)

    def results_send(b, cut):
        for dx, dy in FAR_FIRST:
            d = (px + dx) % WIDE * WIDE + (py + dy) % WIDE
            block_send(b, d, res, back, b_s, b_r, b_l, cut)

    def lanes(cut):
        if cut == 0:
            return pl.ds(0, features)
        return pl.ds((cut - 1) * (features // 2), features // 2)

    def part_out(b, i, cut):
        k = b + max(cut - 1, 0)
        return remote(
            part.at[b, i, :, lanes(cut)], precv.at[b, i, :, lanes(cut)],
            p_s.at[k, i], p_r.at[k, i], sources_of[i],
        )

    def weigh(b):
        for d in range(PLANE):
            pick[d] = jnp.where(
                tgt[b, d:d + 1, :] == places, gat[b, d:d + 1, :], 0.0
            ).astype(BF16)

    def combine(b, cut):
        mixer = pick[...].reshape(PLANE * PAD, LINE * tokens)
        results = back[b, :, :, lanes(cut)]
        width = results.shape[2]
        total = lax.dot_general(
            mixer, results.reshape(PLANE * PAD, width), (((0,), (0,)), ((), ())),
            preferred_element_type=F32,
        ).astype(BF16)
        part[b, :, :, lanes(cut)] = total.reshape(LINE, tokens, width)
        for i in range(1, LINE):
            part_out(b, i, cut).start()

    def finish(b, cut):
        total = part[b, 0, :, lanes(cut)].astype(F32)
        for i in range(1, LINE):
            part_out(b, i, cut).wait_recv()
            total = total + precv[b, i, :, lanes(cut)].astype(F32)
        out[b, :, lanes(cut)] = total

    dispatch(0)
    dispatch(1)
    tick(1)
    for piece in (2, 3, 4, 5, REST, 6):
        tick(piece)
    edge_arrive(1)
    tick(7)
    edge_arrive(3)
    tick(8)

    block_wait(0, outg, recv, a_s, a_r, a_l, "in")
    for m in range(3):
        own_in(m).wait_recv()
        for piece in (4, 8):
            for way in range(2):
                sib(way, piece, m).wait_recv()
    for k in ORDER:
        experts_on(0, zl, k)
    tick(9)
    edge_arrive(5, REST, 7, 9)
    results_send(0, 0)
    block_wait(1, outg, recv, a_s, a_r, a_l, "in")
    for m in range(3):
        for piece in SHARED:
            if piece not in (4, 8):
                for way in range(2):
                    sib(way, piece, m).wait_recv()

    @pl.when(on_edge)
    def _():
        for m in range(3):
            for piece in EDGES:
                esib(piece, m).wait_recv()

    wanted = tnew[e]
    keeps = wanted == told[e]
    lower = wanted == told[(e + experts - 1) % experts]
    bottom = 1 - (zl + HIGH - 1) // HIGH
    column = jnp.where(
        keeps, zl, jnp.where(lower, zl - 1 + bottom * (HIGH + 1), zl + 1)
    )
    for k in ORDER:
        experts_on(1, column, k)
    for cut in (1, 2):
        results_send(1, cut)
    weigh(0)
    block_wait(0, res, back, b_s, b_r, b_l, "in")
    combine(0, 0)
    weigh(1)
    for cut in (1, 2):
        block_wait(1, res, back, b_s, b_r, b_l, "in", cut)
        combine(1, cut)
    finish(0, 0)
    for cut in (1, 2):
        finish(1, cut)

    for m in range(3):
        own(m).wait_send()
        for way in range(2):
            for piece in range(1, REST + 1):
                ring(way, piece, m).wait_send()
            for piece in SHARED:
                sib(way, piece, m).wait_send()

    @pl.when(on_edge)
    def _():
        for m in range(3):
            for piece in EDGES:
                edge(piece, m).wait_send()
                esib(piece, m).wait_send()

    for b in range(2):
        for i in range(1, LINE):
            line_x(b, i).wait_send()
            line_r(b, i).wait_send()
        block_wait(b, outg, recv, a_s, a_r, a_l, "out")
    for b, cut in ((0, 0), (1, 1), (1, 2)):
        for i in range(1, LINE):
            part_out(b, i, cut).wait_send()
        block_wait(b, res, back, b_s, b_r, b_l, "out", cut)


def local(
    batch_one, batch_two, norm_gain, slots_one, slots_two, gates_one, gates_two,
    table_old, table_new, gate_old, up_old, down_old,
):
    tokens, features = batch_one.shape
    shard, inner = gate_old.shape[1:]
    vmem = pl.BlockSpec(memory_space=pltpu.VMEM)
    smem = pl.BlockSpec(memory_space=pltpu.SMEM)
    dma = pltpu.SemaphoreType.DMA
    full = pltpu.VMEM((HIGH + 1, HIGH, 2, shard, inner), BF16)
    blocks = pltpu.VMEM((2, PLANE, PAD, features), BF16)
    line = pltpu.VMEM((2, LINE, tokens, features), BF16)
    mixed = pl.pallas_call(
        body,
        out_shape=jax.ShapeDtypeStruct((2, tokens, features), F32),
        in_specs=[vmem] * 7 + [smem] * 2 + [vmem] * 3,
        out_specs=vmem,
        scratch_shapes=[
            full, full, full,
            line, pltpu.VMEM((2, LINE, 16, tokens), F32),
            blocks, blocks, blocks, blocks,
            pltpu.VMEM((PLANE, PAD, LINE * tokens), BF16),
            line, line,
            pltpu.VMEM((2, PLANE, LINE * tokens), F32), pltpu.VMEM((2, PLANE, LINE * tokens), F32),
            dma((2, REST, 3)), dma((2, REST, 3)), dma((3,)), dma((3,)),
            dma((2, len(SHARED), 3)), dma((2, len(SHARED), 3)),
            dma((6, 3)), dma((6, 3)), dma((6, 3)), dma((6, 3)),
            dma((2, LINE)), dma((2, LINE)), dma((2, LINE)), dma((2, LINE)),
            dma((2, PLANE)), dma((2, PLANE)), dma((2,)),
            dma((3, PLANE)), dma((3, PLANE)), dma((3,)),
            dma((3, LINE)), dma((3, LINE)),
        ],
        compiler_params=pltpu.CompilerParams(
            collective_id=0, has_side_effects=True, vmem_limit_bytes=60 * 1024 * 1024
        ),
    )(
        batch_one, batch_two, norm_gain, slots_one.T, slots_two.T, gates_one.T, gates_two.T,
        table_old, table_new, gate_old[0], up_old[0], down_old[0].T,
    )
    return mixed[0].astype(BF16), mixed[1].astype(BF16)


def solution(mesh):
    rows = P(("expert", "tensor"), None)
    in_specs = (
        rows, rows, P(), rows, rows, rows, rows, P(), P(),
        P("expert", "tensor", None), P("expert", "tensor", None), P("expert", None, "tensor"),
    )
    return jax.shard_map(
        local, mesh=mesh, in_specs=in_specs, out_specs=(rows, rows), check_vma=False
    )
```
